256 devices in a mesh: dp: 16 (over y, x), sub: 16 (over z, core).
Axes of the slice: x: 4, y: 4, z: 8, core: 2. Of those that a mesh axis runs over, the one named last changes fastest.
Arguments:
- embeddings: bfloat16 [49152, 1024], P('dp'), may hold values from -4096 to 4096
- assignment: int32 [49152], P('dp'), may hold values from 0 to 4095
- centroids: bfloat16 [4096, 1024], P('sub'), may hold values from -1 to 1
- codebooks: float32 [64, 16, 256], P('sub'), may hold values from -2 to 2
Outputs:
- new_centroids: float32 [4096, 1024], P('sub')
- new_codebooks: float32 [64, 16, 256], P('sub')
The draws below stay inside these ranges and needn't reach their ends.
All inputs are finite; a program needn't handle non-finite values.
Results may differ from the reference program's by a relative error of at most 0.0004.
The reference program's roundings to bfloat16 on the way count: a program that leaves them out, or rounds other values in their place, can miss the bound.
Values may be sent and summed in bfloat16 or wider, within the bound.
A program may use at most 128 MiB of HBM per device.

```python
import math
import jax
import jax.numpy as jnp
from jax import lax

D = 1024
K = 4096
M = 64
CW = 256
ROW_DEV = 3072
SUB_DIM = 16
ROWS = 49152
N_DP = 16


def joint_draw(key):
    key_list = jax.random.split(jax.random.fold_in(key, 4242), 5)
    assign_ids = jax.random.randint(key_list[0], (ROWS,), 0, K, dtype=jnp.int32)
    cent_scale = 0.6 / math.sqrt(D)
    cent_values = jnp.clip(jax.random.normal(key_list[1], (K, D), jnp.float32), -4.0, 4.0) * cent_scale
    code_values = jnp.clip(jax.random.normal(key_list[2], (M, SUB_DIM, CW), jnp.float32), -6.0, 6.0) * 0.3
    row_scale = jnp.exp(jnp.log(3.0) * jnp.arange(ROWS, dtype=jnp.float32) / ROWS + jax.random.uniform(key_list[3], (ROWS,), jnp.float32, 0.0, math.log(4.0)))
    sample = jnp.clip(jax.random.normal(key_list[4], (ROWS, D), jnp.float32), -4.0, 4.0)
    sample = sample * row_scale[:, None]
    sample = jnp.clip(sample, -4096.0, 4096.0)
    return (sample, assign_ids, cent_values, code_values)


def draw_embeddings(key, part):
    return joint_draw(key)[0].astype(jnp.bfloat16)


def draw_assignment(key, part):
    return joint_draw(key)[1]


def draw_centroids(key, part):
    return joint_draw(key)[2].astype(jnp.bfloat16)


def draw_codebooks(key, part):
    return joint_draw(key)[3]


def setup_inputs(seed: int = 0) -> dict:
    seeds = jax.random.split(jax.random.key(seed), 5)
    return {
        "embeddings": draw_embeddings(jax.random.fold_in(seeds[4], 71), 0),
        "assignment": draw_assignment(jax.random.fold_in(seeds[4], 71), 0),
        "centroids": draw_centroids(jax.random.fold_in(seeds[4], 71), 0),
        "codebooks": draw_codebooks(jax.random.fold_in(seeds[4], 71), 0),
    }


def reference(embeddings, assignment, centroids, codebooks):
    cent_float = centroids.astype(jnp.float32)
    half_norm = 0.5 * jnp.sum(cent_float * cent_float, axis=1)
    code_half = 0.5 * jnp.sum(codebooks * codebooks, axis=1)
    row_tiles = embeddings.reshape(N_DP, ROW_DEV, D)
    tile_ids = assignment.reshape(N_DP, ROW_DEV)

    def accumulate(running, pieces):
        tile_rows, tile_assign = pieces
        logits = jnp.dot(tile_rows, centroids.T, preferred_element_type=jnp.float32) - half_norm[None, :]
        expo_terms = jnp.exp(logits - jnp.max(logits, axis=1, keepdims=True))
        probability = expo_terms / jnp.sum(expo_terms, axis=1, keepdims=True)
        cent_sums = running[0] + jnp.dot(probability.astype(jnp.bfloat16).T, tile_rows, preferred_element_type=jnp.float32)
        cent_counts = running[1] + jnp.sum(probability, axis=0)
        base_rows = jnp.take(centroids, tile_assign.astype(jnp.int32), axis=0).astype(jnp.float32)
        res_parts = (tile_rows.astype(jnp.float32) - base_rows).reshape(ROW_DEV, M, SUB_DIM)
        code_logits = jnp.einsum("rsd,sdc->rsc", res_parts, codebooks, precision=lax.Precision.HIGHEST) - code_half[None]
        code_exp = jnp.exp(code_logits - jnp.max(code_logits, axis=2, keepdims=True))
        code_weights = code_exp / jnp.sum(code_exp, axis=2, keepdims=True)
        code_sums = running[2] + jnp.einsum("rsc,rsd->sdc", code_weights, res_parts, precision=lax.Precision.HIGHEST)
        code_counts = running[3] + jnp.sum(code_weights, axis=0)
        return (cent_sums, cent_counts, code_sums, code_counts), None

    initial = (jnp.zeros((K, D), jnp.float32), jnp.zeros((K,), jnp.float32),
               jnp.zeros((M, SUB_DIM, CW), jnp.float32), jnp.zeros((M, CW), jnp.float32))
    final_state, unused = lax.scan(accumulate, initial, (row_tiles, tile_ids))
    new_centroids = (final_state[0] + cent_float) / (final_state[1][:, None] + 1.0)
    new_codebooks = (final_state[2] + codebooks) / (final_state[3][:, None, :] + 1.0)
    return new_centroids, new_codebooks
```

```python
import jax
import jax.numpy as jnp
from jax import lax
from jax.experimental import pallas as pl
from jax.experimental.pallas import tpu as pltpu
from jax.sharding import PartitionSpec as P

R, D, KL = 3072, 1024, 256
NC, RC = 6, 512
CH = 256
F32, BF16 = jnp.float32, jnp.bfloat16
LOG2E = 1.4426950408889634


def rcopy(src, dst, ssem, rsem, **where):
    return pltpu.make_async_remote_copy(
        src_ref=src, dst_ref=dst, send_sem=ssem, recv_sem=rsem,
        device_id=where, device_id_type=pl.DeviceIdType.MESH,
    )


def split3(v):
    a = v.astype(BF16).astype(F32)
    r = v - a
    b = r.astype(BF16).astype(F32)
    return a, b, (r - b).astype(BF16).astype(F32)


def kernel(
    emb_hbm, asg_hbm, cent_hbm, cb_hbm, out_ref, cbo_ref,
    emb, asg, cent, cb, eT, wT, st, rs, fs, zbuf, tb, tf, xg, embT, cenT, cbt,
    sums, r1, s1, r2, cg, cc, acc, accT, cs, cr,
    lsem, zs, zr, ts, tr, ps, pr, ss, sr, gs, gr, ns, nr, xs, xr, ks, kr, os, orr,
):
    dp = lax.axis_index("dp")
    sub = lax.axis_index("sub")
    y, x = dp // 4, dp % 4
    z, c = sub // 2, sub % 2
    sends = []

    lc = pltpu.make_async_copy(cent_hbm, cent, lsem.at[6])
    lb = pltpu.make_async_copy(cb_hbm, cb, lsem.at[7])
    la = pltpu.make_async_copy(asg_hbm, asg, lsem.at[8])
    lc.start()
    loads = []
    for k in range(NC):
        sl = pl.ds(k * RC, RC)
        cp = pltpu.make_async_copy(emb_hbm.at[sl, :], emb.at[sl, :], lsem.at[k])
        cp.start()
        loads.append(cp)
    lb.start()
    la.start()

    bar = pltpu.get_barrier_semaphore()
    for k in range(1, 16):
        pl.semaphore_signal(bar, inc=1, device_id={"sub": (sub + k) % 16}, device_id_type=pl.DeviceIdType.MESH)
        pl.semaphore_signal(bar, inc=1, device_id={"dp": (dp + k) % 16}, device_id_type=pl.DeviceIdType.MESH)
    st[...] = jnp.ones(st.shape, F32)
    acc[...] = jnp.zeros(acc.shape, F32)
    lc.wait()
    pl.semaphore_wait(bar, 30)

    zc = []
    rows16 = pl.ds(pl.multiple_of(dp * 16, 16), 16)
    for k in range(1, 8):
        zz = (z + k) % 8
        cp = rcopy(cent.at[rows16, pl.ds(pl.multiple_of(zz * 128, 128), 128)], zbuf.at[z],
                   zs.at[k], zr.at[k], sub=zz * 2 + c)
        cp.start()
        zc.append(cp)
    lanes128 = pl.ds(pl.multiple_of(z * 128, 128), 128)
    zbuf[z] = cent[rows16, lanes128]

    cf = cent[...].astype(F32)
    hn = 0.5 * jnp.sum(cf * cf, axis=1, keepdims=True)
    tc = []
    for k in range(NC):
        loads[k].wait()
        l = lax.dot_general(cent[...], emb[k * RC:(k + 1) * RC, :], (((1,), (1,)), ((), ())),
                            preferred_element_type=F32) - hn
        m = jnp.max(l, axis=0, keepdims=True)
        e = jnp.exp(l - m)
        s = jnp.sum(e, axis=0, keepdims=True)
        eT[:, k * RC:(k + 1) * RC] = e
        for i in range(RC // 128):
            r = k * (RC // 128) + i
            st[r % 16, pl.ds(r // 16, 1), :] = m[:, i * 128:(i + 1) * 128]
            st[r % 16, pl.ds(2 + r // 16, 1), :] = s[:, i * 128:(i + 1) * 128]
        if k == 2:
            for cp in zc:
                cp.wait()
            tb[:, c, dp] = zbuf[...]
            for j in range(1, 16):
                cp = rcopy(zbuf, tb.at[:, c, dp], ts.at[j], tr.at[j], dp=(dp + j) % 16)
                cp.start()
                tc.append(cp)

    sc_ = []
    for k in range(1, 16):
        o = (sub + k) % 16
        cp = rcopy(st.at[o], rs.at[sub], ss.at[k], sr.at[k], sub=o)
        cp.start()
        sc_.append(cp)
    rs[sub] = st[sub]

    lb.wait()
    for s in range(4):
        v = cb[s]
        parts = split3(v * LOG2E)
        half = split3(-0.5 * LOG2E * jnp.sum(v * v, axis=0, keepdims=True))
        neg = tuple(-p for p in parts)
        stack = jnp.concatenate(parts + neg + half + (jnp.zeros((29, 256), F32),), axis=0)
        cbt[s] = jnp.transpose(stack).astype(BF16)

    for cp in sc_:
        cp.wait()
    v = rs[...]
    big = jnp.max(v[:, 0:2], axis=0)
    tot = jnp.sum(v[:, 2:4] * jnp.exp(v[:, 0:2] - big[None]), axis=0)
    fs[sub, 0:2, :] = big
    fs[sub, 2:4, :] = tot
    fc = []
    for k in range(1, 16):
        cp = rcopy(fs.at[sub], fs.at[sub], gs.at[k], gr.at[k], sub=(sub + k) % 16)
        cp.start()
        fc.append(cp)

    def turn(k, _):
        o = pl.multiple_of(k * RC, RC)
        embT[:, pl.ds(o, RC)] = jnp.transpose(emb[pl.ds(o, RC), lanes128].astype(F32)).astype(BF16)
        return 0
    lax.fori_loop(0, NC, turn, 0)

    for cp in fc:
        cp.wait()
    cp_ = jnp.zeros((KL, 128), F32)
    for k in range(NC):
        scale = []
        for i in range(RC // 128):
            r = k * (RC // 128) + i
            a, b = r % 16, r // 16
            scale.append(jnp.exp(st[a, pl.ds(b, 1), :] - fs[a, pl.ds(b, 1), :]) / fs[a, pl.ds(2 + b, 1), :])
        p = eT[:, k * RC:(k + 1) * RC] * jnp.concatenate(scale, axis=1)
        for i in range(RC // 128):
            cp_ = cp_ + p[:, i * 128:(i + 1) * 128]
        wT[:, k * RC:(k + 1) * RC] = p.astype(BF16)

    ax = [(x, y), (x, y), (y, x), (y, x)]

    def peer(q, first, k):
        ix, iy = x, y
        if (q < 2) == first:
            ix = (x + k) % 4
        else:
            iy = (y + k) % 4
        return iy * 4 + ix, (ix if (q < 2) == first else iy)

    c1 = [[] for _ in range(4)]
    for q in range(4):
        sums[q] = jnp.dot(wT[...], emb[:, q * 256:(q + 1) * 256], preferred_element_type=F32)
        for k in range(1, 4):
            dev, pa = peer(q, True, k)
            cp = rcopy(sums.at[q, pl.ds(pl.multiple_of(pa * 64, 64), 64), :], r1.at[q, k - 1],
                       xs.at[0, q, k], xr.at[0, q, k], dp=dev)
            cp.start()
            c1[q].append(cp)

    cg[dp] = jnp.broadcast_to(jnp.sum(jnp.transpose(cp_), axis=0, keepdims=True), (8, 256))
    nc = []
    for k in range(1, 16):
        cp = rcopy(cg.at[dp], cg.at[dp], ns.at[k], nr.at[k], dp=(dp + k) % 16)
        cp.start()
        nc.append(cp)

    for cp in tc:
        cp.wait()
    cp = rcopy(tb.at[:, c], tb.at[:, c], ps.at[0], pr.at[0], sub=z * 2 + (1 - c))
    cp.start()
    cp.wait()
    la.wait()

    def widen(i, _):
        tf[pl.ds(pl.multiple_of(i * 256, 256), 256), :] = tb[i // 2, i % 2].reshape(256, 128).astype(F32)
        return 0
    lax.fori_loop(0, 16, widen, 0)

    def fetch(i, _):
        o = pl.multiple_of(i * 16, 16)
        for j in range(16):
            xg[pl.ds(o + j, 1), :] = tf[pl.ds(asg[o + j], 1), :]
        return 0
    lax.fori_loop(0, R // 16, fetch, 0)

    c2 = [[] for _ in range(4)]
    for q in range(4):
        for cp in c1[q]:
            cp.wait()
        a, b = ax[q]
        s1[q] = sums[q, pl.ds(pl.multiple_of(a * 64, 64), 64), :] + r1[q, 0] + r1[q, 1] + r1[q, 2]
        for k in range(1, 4):
            dev, pb = peer(q, False, k)
            cp = rcopy(s1.at[q, pl.ds(pl.multiple_of(pb * 16, 16), 16), :], r2.at[q, k - 1],
                       xs.at[1, q, k], xr.at[1, q, k], dp=dev)
            cp.start()
            c2[q].append(cp)

    mine = (lax.broadcasted_iota(jnp.int32, (RC, 128), 1) // 64) == c

    def turn2(k, _):
        o = pl.multiple_of(k * RC, RC)
        g = xg[pl.ds(o, RC), :]
        cenT[:, pl.ds(o, RC)] = jnp.transpose(g).astype(BF16)
        xg[pl.ds(o, RC), :] = jnp.where(mine, g, 1.0)
        return 0
    lax.fori_loop(0, NC, turn2, 0)

    feats = pl.ds(pl.multiple_of(c * 64, 64), 64)

    def code(k, _):
        o = pl.multiple_of(k * CH, CH)
        et = embT[feats, pl.ds(o, CH)]
        ct = cenT[feats, pl.ds(o, CH)]
        xr_ = jnp.concatenate([emb[pl.ds(o, CH), lanes128], xg[pl.ds(o, CH), :].astype(BF16)], axis=1)
        one = jnp.ones((16, CH), BF16)
        for s in range(4):
            es, cs_ = et[16 * s:16 * s + 16], ct[16 * s:16 * s + 16]
            xt = jnp.concatenate([es, es, es, cs_, cs_, cs_, one, one], axis=0)
            l = jnp.dot(cbt[s], xt, preferred_element_type=F32)
            e = jnp.exp2(l - jnp.max(l, axis=0, keepdims=True))
            w = e * (1.0 / jnp.sum(e, axis=0, keepdims=True))
            hi = w.astype(BF16)
            lo = (w - hi.astype(F32)).astype(BF16)
            acc[s] += jnp.dot(hi, xr_, preferred_element_type=F32) + jnp.dot(lo, xr_, preferred_element_type=F32)
        return 0

    lax.fori_loop(0, 4, code, 0)

    for cp in nc:
        cp.wait()
    ctot = jnp.sum(cg[...], axis=0)[0:1]
    cc[...] = jnp.transpose(jnp.broadcast_to(ctot, (128, 256))) + 1.0
    c3 = [[] for _ in range(4)]
    for q in range(4):
        for cp in c2[q]:
            cp.wait()
        a, b = ax[q]
        row = pl.ds(pl.multiple_of(a * 64 + b * 16, 16), 16)
        qs = slice(q * 256, (q + 1) * 256)
        fin = s1[q, pl.ds(pl.multiple_of(b * 16, 16), 16), :] + r2[q, 0] + r2[q, 1] + r2[q, 2]
        den = cc[row, :]
        out_ref[row, qs] = (fin + cent[row, qs].astype(F32)) / jnp.concatenate([den, den], axis=1)
        for k in range(1, 4):
            dev, _ = peer(q, False, k)
            piece = out_ref.at[row, pl.ds(q * 256, 256)]
            cp = rcopy(piece, piece, xs.at[2, q, k], xr.at[2, q, k], dp=dev)
            cp.start()
            c3[q].append(cp)

    lax.fori_loop(4, 7, code, 0)

    c4 = []
    for q in range(4):
        for cp in c3[q]:
            cp.wait()
        a, b = ax[q]
        for k in range(1, 4):
            dev, _ = peer(q, True, k)
            piece = out_ref.at[pl.ds(pl.multiple_of(a * 64, 64), 64), pl.ds(q * 256, 256)]
            cp = rcopy(piece, piece, xs.at[3, q, k], xr.at[3, q, k], dp=dev)
            cp.start()
            c4.append(cp)

    lax.fori_loop(7, R // CH, code, 0)

    for s in range(4):
        accT[...] = jnp.transpose(acc[s])
        f = pl.multiple_of(c * 64 + s * 16, 16)
        tot16 = accT[pl.ds(f, 16), :] - accT[pl.ds(pl.multiple_of(128 + f, 16), 16), :]
        cnt = accT[pl.ds(pl.multiple_of(128 + (1 - c) * 64, 64), 8), :]
        for h in range(2):
            for g in range(2):
                cs[s * 4 + h * 2 + g, 0:8, :] = tot16[8 * g:8 * g + 8, 128 * h:128 * h + 128]
                cs[s * 4 + h * 2 + g, 8:16, :] = cnt[:, 128 * h:128 * h + 128]
    kc = []
    for k in range(1, 16):
        o = (dp + k) % 16
        cp = rcopy(cs.at[o], cr.at[dp], ks.at[k], kr.at[k], dp=o)
        cp.start()
        kc.append(cp)
    cr[dp] = cs[dp]
    for cp in kc:
        cp.wait()
    t = jnp.sum(cr[...], axis=0)
    so, ho, go = dp // 4, (dp // 2) % 2, dp % 2
    g8 = pl.ds(pl.multiple_of(go * 8, 8), 8)
    h128 = pl.ds(pl.multiple_of(ho * 128, 128), 128)
    cbo_ref[so, g8, h128] = (t[0:8] + cb[so, g8, h128]) / (t[8:16] + 1.0)
    oc = []
    for k in range(1, 16):
        piece = cbo_ref.at[so, g8, h128]
        cp = rcopy(piece, piece, os.at[k], orr.at[k], dp=(dp + k) % 16)
        cp.start()
        oc.append(cp)
    for cp in c4 + oc:
        cp.wait()


def shards(embeddings, assignment, centroids, codebooks):
    dma = pltpu.SemaphoreType.DMA
    v = pltpu.VMEM
    hbm = pl.BlockSpec(memory_space=pl.ANY)
    vm = pl.BlockSpec(memory_space=pltpu.VMEM)
    return pl.pallas_call(
        kernel,
        out_shape=(jax.ShapeDtypeStruct((KL, D), F32), jax.ShapeDtypeStruct((4, 16, 256), F32)),
        in_specs=[hbm] * 4,
        out_specs=(vm, vm),
        scratch_shapes=[
            v((R, D), BF16), pltpu.SMEM((R,), jnp.int32), v((KL, D), BF16), v((4, 16, 256), F32),
            v((KL, R), F32), v((KL, R), BF16),
            v((16, 8, 128), F32), v((16, 8, 128), F32), v((16, 8, 128), F32),
            v((8, 16, 128), BF16), v((8, 2, 16, 16, 128), BF16), v((4096, 128), F32), v((R, 128), F32),
            v((128, R), BF16), v((128, R), BF16), v((4, 256, 128), BF16),
            v((4, 256, 256), F32), v((4, 3, 64, 256), F32), v((4, 64, 256), F32), v((4, 3, 16, 256), F32),
            v((16, 8, 256), F32), v((256, 128), F32), v((4, 256, 256), F32), v((256, 256), F32),
            v((16, 16, 128), F32), v((16, 16, 128), F32),
            dma((9,)), dma((8,)), dma((8,)), dma((16,)), dma((16,)), dma((1,)), dma((1,)),
            dma((16,)), dma((16,)), dma((16,)), dma((16,)), dma((16,)), dma((16,)),
            dma((4, 4, 4)), dma((4, 4, 4)), dma((16,)), dma((16,)), dma((16,)), dma((16,)),
        ],
        compiler_params=pltpu.CompilerParams(
            collective_id=0, has_side_effects=True, vmem_limit_bytes=52 * 1024 * 1024),
        name="step",
    )(embeddings, assignment, centroids, codebooks)


def solution(mesh):
    placed = (P("dp", None), P("dp"), P("sub", None), P("sub", None, None))
    return jax.shard_map(
        shards,
        mesh=mesh,
        in_specs=placed,
        out_specs=(P("sub", None), P("sub", None, None)),
        check_vma=False,
    )
```

```python
import jax
import jax.numpy as jnp
from jax import lax
from jax.experimental import pallas as pl
from jax.experimental.pallas import tpu as pltpu
from jax.sharding import PartitionSpec as P

R, D, KL = 3072, 1024, 256
NC, RC = 6, 512
F32, BF16 = jnp.float32, jnp.bfloat16
LOG2E = 1.4426950408889634


def rcopy(src, dst, ssem, rsem, **where):
    return pltpu.make_async_remote_copy(
        src_ref=src, dst_ref=dst, send_sem=ssem, recv_sem=rsem,
        device_id=where, device_id_type=pl.DeviceIdType.MESH,
    )


def split3(v):
    a = v.astype(BF16).astype(F32)
    r = v - a
    b = r.astype(BF16).astype(F32)
    return a, b, (r - b).astype(BF16).astype(F32)


def kernel(
    emb_hbm, asg_hbm, cent_hbm, cb_hbm, out_ref, cbo_ref,
    emb, asg, cent, cb, eT, wT, st, ra, mz, fs, scl, zbuf, tb, tf, xg, embT, cenT, cbt,
    sums, r1, s1, r2, cg, cc, acc, accT, cs, cr, xgb, lsc, wh,
    lsem, zs, zr, ts, tr, ps, pr, ss, sr, gs, gr, ns, nr, xs, xr, ks, kr, os, orr,
):
    dp = lax.axis_index("dp")
    sub = lax.axis_index("sub")
    y, x = dp // 4, dp % 4
    z, c = sub // 2, sub % 2

    with jax.named_scope("load"):
        lc = pltpu.make_async_copy(cent_hbm, cent, lsem.at[6])
        lb = pltpu.make_async_copy(cb_hbm, cb, lsem.at[7])
        la = pltpu.make_async_copy(asg_hbm, asg, lsem.at[8])
        lc.start()
        loads = []
        for k in range(3):
            sl = pl.ds(k * 1024, 1024)
            cp = pltpu.make_async_copy(emb_hbm.at[sl, :], emb.at[sl, :], lsem.at[k])
            cp.start()
            loads.append(cp)
        lb.start()
        la.start()
        bar = pltpu.get_barrier_semaphore()
        for k in range(1, 16):
            pl.semaphore_signal(bar, inc=1, device_id={"sub": (sub + k) % 16}, device_id_type=pl.DeviceIdType.MESH)
            pl.semaphore_signal(bar, inc=1, device_id={"dp": (dp + k) % 16}, device_id_type=pl.DeviceIdType.MESH)
        acc[...] = jnp.zeros(acc.shape, F32)
        rows16 = pl.ds(pl.multiple_of(dp * 16, 16), 16)
        lanes128 = pl.ds(pl.multiple_of(z * 128, 128), 128)
        lc.wait()
        zbuf[z] = cent[rows16, lanes128]

    with jax.named_scope("logits"):
        cf = cent[...].astype(F32)
        hn = 0.5 * jnp.sum(cf * cf, axis=1, keepdims=True)
        for k in range(NC):
            if k % 2 == 0:
                loads[k // 2].wait()
            l = lax.dot_general(cent[...], emb[k * RC:(k + 1) * RC, :], (((1,), (1,)), ((), ())),
                                preferred_element_type=F32) - hn
            m = jnp.max(l, axis=0, keepdims=True)
            e = jnp.exp(l - m)
            s = jnp.sum(e, axis=0, keepdims=True)
            eT[:, k * RC:(k + 1) * RC] = e
            for i in range(RC // 128):
                h, r = divmod(k * (RC // 128) + i, 12)
                st[h, r:r + 1, :] = m[:, i * 128:(i + 1) * 128]
                st[h, 12 + r:13 + r, :] = s[:, i * 128:(i + 1) * 128]

    with jax.named_scope("barrier"):
        pl.semaphore_wait(bar, 30)
    with jax.named_scope("statsend"):
        other = z * 2 + (1 - c)
        ca = rcopy(st.at[1 - c], ra, ss.at[0], sr.at[0], sub=other)
        ca.start()
    with jax.named_scope("zsend"):
        zc = []
        for k in range(1, 8):
            zz = (z + k) % 8
            cp = rcopy(cent.at[rows16, pl.ds(pl.multiple_of(zz * 128, 128), 128)], zbuf.at[z],
                       zs.at[k], zr.at[k], sub=zz * 2 + c)
            cp.start()
            zc.append(cp)
    with jax.named_scope("cbprep"):
        lb.wait()
        for s in range(4):
            v = cb[s]
            parts = split3(v * LOG2E)
            half = split3(-0.5 * LOG2E * jnp.sum(v * v, axis=0, keepdims=True))
            neg = tuple(-p for p in parts)
            stack = jnp.concatenate(parts + neg + half + (jnp.zeros((29, 256), F32),), axis=0)
            cbt[s] = jnp.transpose(stack).astype(BF16)
        for k in range(NC):
            o = k * RC
            embT[:, pl.ds(o, RC)] = jnp.transpose(emb[pl.ds(o, RC), lanes128].astype(F32)).astype(BF16)

    with jax.named_scope("statwait"):
        ca.wait()
    with jax.named_scope("merge"):
        ma, mb = st[c, 0:12, :], ra[0:12, :]
        big = jnp.maximum(ma, mb)
        mz[z, 0:12, :] = big
        mz[z, 12:24, :] = st[c, 12:24, :] * jnp.exp(ma - big) + ra[12:24, :] * jnp.exp(mb - big)
        bc = []
        for k in range(1, 8):
            cp = rcopy(mz.at[z], mz.at[z], gs.at[k], gr.at[k], sub=((z + k) % 8) * 2 + c)
            cp.start()
            bc.append(cp)
    with jax.named_scope("zwait"):
        for cp in zc:
            cp.wait()
    with jax.named_scope("tabsend"):
        tb[:, c, dp] = zbuf[...]
        tc = []
        for j in range(1, 16):
            cp = rcopy(zbuf, tb.at[:, c, dp], ts.at[j], tr.at[j], dp=(dp + j) % 16)
            cp.start()
            tc.append(cp)
    with jax.named_scope("finwait"):
        for cp in bc:
            cp.wait()
    with jax.named_scope("merge2"):
        mv = mz[:, 0:12, :]
        big = jnp.max(mv, axis=0)
        fs[c, 0:12, :] = big
        fs[c, 12:24, :] = jnp.sum(mz[:, 12:24, :] * jnp.exp(mv - big[None]), axis=0)
        cp = rcopy(fs.at[c], fs.at[c], ss.at[1], sr.at[1], sub=other)
        cp.start()
        cp.wait()
    with jax.named_scope("weights"):
        cp_ = jnp.zeros((KL, 128), F32)
        for h in range(2):
            scl[h] = jnp.exp(st[h, 0:12, :] - fs[h, 0:12, :]) / fs[h, 12:24, :]
        for k in range(NC):
            scale = []
            for i in range(RC // 128):
                h, r = divmod(k * (RC // 128) + i, 12)
                scale.append(scl[h, r:r + 1, :])
            p = eT[:, k * RC:(k + 1) * RC] * jnp.concatenate(scale, axis=1)
            for i in range(RC // 128):
                cp_ = cp_ + p[:, i * 128:(i + 1) * 128]
            wT[:, k * RC:(k + 1) * RC] = p.astype(BF16)
    with jax.named_scope("sums"):
        ax = [(x, y), (x, y), (y, x), (y, x)]

        def peer(q, first, k):
            ix, iy = x, y
            if (q < 2) == first:
                ix = (x + k) % 4
            else:
                iy = (y + k) % 4
            return iy * 4 + ix, (ix if (q < 2) == first else iy)

        c1 = [[] for _ in range(4)]
        for q in (0, 2, 1, 3):
            sums[q] = jnp.dot(wT[...], emb[:, q * 256:(q + 1) * 256], preferred_element_type=F32)
        for q in (0, 2, 1, 3):
            for k in range(1, 4):
                dev, pa = peer(q, True, k)
                cp = rcopy(sums.at[q, pl.ds(pl.multiple_of(pa * 64, 64), 64), :], r1.at[q, k - 1],
                           xs.at[0, q, k], xr.at[0, q, k], dp=dev)
                cp.start()
                c1[q].append(cp)
    with jax.named_scope("counts"):
        cg[dp] = jnp.broadcast_to(jnp.sum(jnp.transpose(cp_), axis=0, keepdims=True), (8, 256))
        nc = []
        for k in range(1, 16):
            cp = rcopy(cg.at[dp], cg.at[dp], ns.at[k], nr.at[k], dp=(dp + k) % 16)
            cp.start()
            nc.append(cp)

    with jax.named_scope("tabwait"):
        pc = []
        for j in range(16):
            if j:
                tc[j - 1].wait()
            dd = (dp + 16 - j) % 16
            cp = rcopy(tb.at[:, c, dd], tb.at[:, c, dd], ps.at[j], pr.at[j], sub=z * 2 + (1 - c))
            cp.start()
            pc.append(cp)
    with jax.named_scope("swap"):
        for cp in pc:
            cp.wait()
        la.wait()
    with jax.named_scope("widen"):
        for i in range(16):
            tf[pl.ds(i * 256, 256), :] = tb[i // 2, i % 2].reshape(256, 128).astype(F32)
    with jax.named_scope("gather"):
        def fetch(i, _):
            o = pl.multiple_of(i * 32, 32)
            for j in range(32):
                xg[pl.ds(o + j, 1), :] = tf[pl.ds(asg[o + j], 1), :]
            return 0
        lax.fori_loop(0, R // 32, fetch, 0)

    with jax.named_scope("stage1"):
        c2 = [[] for _ in range(4)]
        for q in (0, 2, 1, 3):
            for cp in c1[q]:
                cp.wait()
            a, b = ax[q]
            s1[q] = sums[q, pl.ds(pl.multiple_of(a * 64, 64), 64), :] + r1[q, 0] + r1[q, 1] + r1[q, 2]
            for k in range(1, 4):
                dev, pb = peer(q, False, k)
                cp = rcopy(s1.at[q, pl.ds(pl.multiple_of(pb * 16, 16), 16), :], r2.at[q, k - 1],
                           xs.at[1, q, k], xr.at[1, q, k], dp=dev)
                cp.start()
                c2[q].append(cp)

    with jax.named_scope("turn2"):
        mine = (lax.broadcasted_iota(jnp.int32, (RC, 128), 1) // 64) == c
        for k in range(NC):
            g = xg[pl.ds(k * RC, RC), :]
            cenT[:, pl.ds(k * RC, RC)] = jnp.transpose(g).astype(BF16)
            xgb[pl.ds(k * RC, RC), :] = jnp.where(mine, g, 1.0).astype(BF16)

    one = jnp.ones((16, RC), BF16)

    def code_logits(i):
        k, s = i // 4, i % 4
        cols = pl.ds(k * RC, RC)
        f = pl.ds(pl.multiple_of(c * 64 + 16 * s, 16), 16)
        es, cs_ = embT[f, cols], cenT[f, cols]
        xt = jnp.concatenate([es, es, es, cs_, cs_, cs_, one, one], axis=0)
        lsc[i % 2] = jnp.dot(cbt[s], xt, preferred_element_type=F32)

    def code(lo_, hi_):
        for i in range(lo_, hi_):
            k, s = i // 4, i % 4
            if i + 1 < 4 * NC:
                code_logits(i + 1)
            for j in range(RC // 256):
                l = lsc[i % 2, :, j * 256:(j + 1) * 256]
                e = jnp.exp2(l - jnp.max(l, axis=0, keepdims=True))
                w = e * (1.0 / jnp.sum(e, axis=0, keepdims=True))
                hi = w.astype(BF16)
                wh[s, :, j * 256:(j + 1) * 256] = hi
                wh[s, :, RC + j * 256:RC + (j + 1) * 256] = (w - hi.astype(F32)).astype(BF16)
            rows = pl.ds(k * RC, RC)
            both = jnp.concatenate([emb[rows, lanes128], xgb[rows, :]], axis=1)
            acc[s] += (jnp.dot(wh[s, :, 0:RC], both, preferred_element_type=F32)
                       + jnp.dot(wh[s, :, RC:2 * RC], both, preferred_element_type=F32))

    with jax.named_scope("code1"):
        code_logits(0)
        code(0, 12)

    with jax.named_scope("cntwait"):
        for cp in nc:
            cp.wait()
        ctot = jnp.sum(cg[...], axis=0)[0:1]
        cc[...] = jnp.transpose(jnp.broadcast_to(ctot, (128, 256))) + 1.0
    with jax.named_scope("stage2"):
        c3 = [[] for _ in range(4)]
        for q in (0, 2, 1, 3):
            for cp in c2[q]:
                cp.wait()
            a, b = ax[q]
            row = pl.ds(pl.multiple_of(a * 64 + b * 16, 16), 16)
            qs = slice(q * 256, (q + 1) * 256)
            fin = s1[q, pl.ds(pl.multiple_of(b * 16, 16), 16), :] + r2[q, 0] + r2[q, 1] + r2[q, 2]
            den = cc[row, :]
            out_ref[row, qs] = (fin + cent[row, qs].astype(F32)) / jnp.concatenate([den, den], axis=1)
            for k in range(1, 4):
                dev, _ = peer(q, False, k)
                piece = out_ref.at[row, pl.ds(q * 256, 256)]
                cp = rcopy(piece, piece, xs.at[2, q, k], xr.at[2, q, k], dp=dev)
                cp.start()
                c3[q].append(cp)

    with jax.named_scope("code2"):
        code(12, 4 * NC)

    with jax.named_scope("codeprep"):
        for s in range(4):
            accT[...] = jnp.transpose(acc[s])
            f = pl.multiple_of(c * 64 + s * 16, 16)
            tot16 = accT[pl.ds(f, 16), :] - accT[pl.ds(pl.multiple_of(128 + f, 16), 16), :]
            cnt = accT[pl.ds(pl.multiple_of(128 + (1 - c) * 64, 64), 8), :]
            for h in range(2):
                for g in range(2):
                    cs[s * 4 + h * 2 + g, 0:8, :] = tot16[8 * g:8 * g + 8, 128 * h:128 * h + 128]
                    cs[s * 4 + h * 2 + g, 8:16, :] = cnt[:, 128 * h:128 * h + 128]
    with jax.named_scope("codesend"):
        kc = []
        for k in range(1, 16):
            o = (dp + k) % 16
            cp = rcopy(cs.at[o], cr.at[dp], ks.at[k], kr.at[k], dp=o)
            cp.start()
            kc.append(cp)
        cr[dp] = cs[dp]
    with jax.named_scope("stage3"):
        c4 = []
        for q in (0, 2, 1, 3):
            for cp in c3[q]:
                cp.wait()
            a, b = ax[q]
            for k in range(1, 4):
                dev, _ = peer(q, True, k)
                piece = out_ref.at[pl.ds(pl.multiple_of(a * 64, 64), 64), pl.ds(q * 256, 256)]
                cp = rcopy(piece, piece, xs.at[3, q, k], xr.at[3, q, k], dp=dev)
                cp.start()
                c4.append(cp)

    with jax.named_scope("codewait"):
        for cp in kc:
            cp.wait()
    with jax.named_scope("codefin"):
        t = jnp.sum(cr[...], axis=0)
        so, ho, go = dp // 4, (dp // 2) % 2, dp % 2
        g8 = pl.ds(pl.multiple_of(go * 8, 8), 8)
        h128 = pl.ds(pl.multiple_of(ho * 128, 128), 128)
        cbo_ref[so, g8, h128] = (t[0:8] + cb[so, g8, h128]) / (t[8:16] + 1.0)
        oc = []
        for k in range(1, 16):
            piece = cbo_ref.at[so, g8, h128]
            cp = rcopy(piece, piece, os.at[k], orr.at[k], dp=(dp + k) % 16)
            cp.start()
            oc.append(cp)
    with jax.named_scope("newcent"):
        for cp in c4:
            cp.wait()
    with jax.named_scope("newcode"):
        for cp in oc:
            cp.wait()


def shards(embeddings, assignment, centroids, codebooks):
    dma = pltpu.SemaphoreType.DMA
    v = pltpu.VMEM
    hbm = pl.BlockSpec(memory_space=pltpu.HBM)
    vm = pl.BlockSpec(memory_space=pltpu.VMEM)
    return pl.pallas_call(
        kernel,
        out_shape=(v((KL, D), F32), v((4, 16, 256), F32)),
        in_specs=[hbm] * 4,
        out_specs=(vm, vm),
        scratch_shapes=[
            v((R, D), BF16), pltpu.SMEM((R,), jnp.int32), v((KL, D), BF16), v((4, 16, 256), F32),
            v((KL, R), F32), v((KL, R), BF16),
            v((2, 24, 128), F32), v((24, 128), F32), v((8, 24, 128), F32), v((2, 24, 128), F32), v((2, 12, 128), F32),
            v((8, 16, 128), BF16), v((8, 2, 16, 16, 128), BF16), v((4096, 128), F32), v((R, 128), F32),
            v((128, R), BF16), v((128, R), BF16), v((4, 256, 128), BF16),
            v((4, 256, 256), F32), v((4, 3, 64, 256), F32), v((4, 64, 256), F32), v((4, 3, 16, 256), F32),
            v((16, 8, 256), F32), v((256, 128), F32), v((4, 256, 256), F32), v((256, 256), F32),
            v((16, 16, 128), F32), v((16, 16, 128), F32),
            v((R, 128), BF16), v((2, 256, RC), F32), v((4, 256, 2 * RC), BF16),
            dma((9,)), dma((8,)), dma((8,)), dma((16,)), dma((16,)), dma((16,)), dma((16,)),
            dma((16,)), dma((16,)), dma((16,)), dma((16,)), dma((16,)), dma((16,)),
            dma((4, 4, 4)), dma((4, 4, 4)), dma((16,)), dma((16,)), dma((16,)), dma((16,)),
        ],
        compiler_params=pltpu.CompilerParams(
            collective_id=0, has_side_effects=True, vmem_limit_bytes=60 * 1024 * 1024),
        name="step",
    )(*(pltpu.with_memory_space_constraint(a, pltpu.HBM) for a in (embeddings, assignment, centroids, codebooks)))


def solution(mesh):
    placed = (P("dp", None), P("dp"), P("sub", None), P("sub", None, None))
    return jax.shard_map(
        shards,
        mesh=mesh,
        in_specs=placed,
        out_specs=(P("sub", None), P("sub", None, None)),
        check_vma=False,
    )
```

```python
import jax
import jax.numpy as jnp
from jax import lax
from jax.experimental import pallas as pl
from jax.experimental.pallas import tpu as pltpu
from jax.sharding import PartitionSpec as P

R, D, KL = 3072, 1024, 256
NC, RC = 6, 512
PAIR, BACK, ZFAR, ZNEAR, TAB, SWAP, SWAP2, OVERZ, COUNT, CODE, NEWCODE, CENT = range(12)
PHASES = CENT + 8
F32, BF16 = jnp.float32, jnp.bfloat16
LOG2E = 1.4426950408889634


def rcopy(src, dst, ssem, rsem, **where):
    return pltpu.make_async_remote_copy(
        src_ref=src, dst_ref=dst, send_sem=ssem, recv_sem=rsem,
        device_id=where, device_id_type=pl.DeviceIdType.MESH,
    )


def drain(ref, sem):
    pltpu.make_async_copy(ref, ref, sem).wait()


def split3(v):
    a = v.astype(BF16).astype(F32)
    r = v - a
    b = r.astype(BF16).astype(F32)
    return a, b, (r - b).astype(BF16).astype(F32)


def kernel(
    emb_hbm, asg_hbm, cent_hbm, cb_hbm, out_ref, cbo_ref,
    emb, asg, cent, cb, eT, wT, st, ra, mz, fs, scl, zbuf, tb, tf, xg, embT, cenT, cbt,
    sums, r1, s1, r2, cg, cc, acc, accT, cs, cr, xgb, lsc, wh,
    lsem, snd, rcv,
):
    dp = lax.axis_index("dp")
    sub = lax.axis_index("sub")
    y, x = dp // 4, dp % 4
    z, c = sub // 2, sub % 2

    def send(phase, src, dst, **where):
        rcopy(src, dst, snd.at[phase], rcv.at[phase], **where).start()

    with jax.named_scope("load"):
        lc = pltpu.make_async_copy(cent_hbm, cent, lsem.at[3])
        lb = pltpu.make_async_copy(cb_hbm, cb, lsem.at[4])
        la = pltpu.make_async_copy(asg_hbm, asg, lsem.at[5])
        lc.start()
        loads = []
        for k in range(3):
            sl = pl.ds(k * 1024, 1024)
            cp = pltpu.make_async_copy(emb_hbm.at[sl, :], emb.at[sl, :], lsem.at[k])
            cp.start()
            loads.append(cp)
        lb.start()
        la.start()
        bar = pltpu.get_barrier_semaphore()
        for k in range(1, 16):
            pl.semaphore_signal(bar, inc=1, device_id={"sub": (sub + k) % 16}, device_id_type=pl.DeviceIdType.MESH)
            pl.semaphore_signal(bar, inc=1, device_id={"dp": (dp + k) % 16}, device_id_type=pl.DeviceIdType.MESH)
        acc[...] = jnp.zeros(acc.shape, F32)
        rows16 = pl.ds(pl.multiple_of(dp * 16, 16), 16)
        lanes128 = pl.ds(pl.multiple_of(z * 128, 128), 128)
        lc.wait()
        tb[0, c] = cent[:, lanes128]

    with jax.named_scope("logits"):
        cf = cent[...].astype(F32)
        hn = 0.5 * jnp.sum(cf * cf, axis=1, keepdims=True)
        for k in range(NC):
            if k % 2 == 0:
                loads[k // 2].wait()
            l = lax.dot_general(cent[...], emb[k * RC:(k + 1) * RC, :], (((1,), (1,)), ((), ())),
                                preferred_element_type=F32) - hn
            m = jnp.max(l, axis=0, keepdims=True)
            e = jnp.exp(l - m)
            s = jnp.sum(e, axis=0, keepdims=True)
            eT[:, k * RC:(k + 1) * RC] = e
            for i in range(RC // 128):
                h, r = divmod(k * (RC // 128) + i, 12)
                st[h, r:r + 1, :] = m[:, i * 128:(i + 1) * 128]
                st[h, 12 + r:13 + r, :] = s[:, i * 128:(i + 1) * 128]

    with jax.named_scope("barrier"):
        pl.semaphore_wait(bar, 30)
    with jax.named_scope("statsend"):
        other = z * 2 + (1 - c)
        send(PAIR, st.at[1 - c], ra, sub=other)
    with jax.named_scope("zsend"):
        for k in range(3, 6):
            zz = (z + k) % 8
            send(ZFAR, cent.at[rows16, pl.ds(pl.multiple_of(zz * 128, 128), 128)], zbuf.at[5 - k], sub=zz * 2 + c)
    with jax.named_scope("cbprep"):
        lb.wait()
        for s in range(4):
            v = cb[s]
            parts = split3(v * LOG2E)
            half = split3(-0.5 * LOG2E * jnp.sum(v * v, axis=0, keepdims=True))
            neg = tuple(-p for p in parts)
            stack = jnp.concatenate(parts + neg + half + (jnp.zeros((29, 256), F32),), axis=0)
            cbt[s] = jnp.transpose(stack).astype(BF16)
        for k in range(NC):
            o = k * RC
            embT[:, pl.ds(o, RC)] = jnp.transpose(emb[pl.ds(o, RC), lanes128].astype(F32)).astype(BF16)

    with jax.named_scope("statwait"):
        drain(ra, rcv.at[PAIR])
    with jax.named_scope("merge"):
        ma, mb = st[c, 0:12, :], ra[0:12, :]
        big = jnp.maximum(ma, mb)
        mz[z, 0:12, :] = big
        mz[z, 12:24, :] = st[c, 12:24, :] * jnp.exp(ma - big) + ra[12:24, :] * jnp.exp(mb - big)
        for k in range(1, 8):
            send(OVERZ, mz.at[z], mz.at[z], sub=((z + k) % 8) * 2 + c)
        for k in (1, 7, 2, 6):
            zz = (z + k) % 8
            send(ZNEAR, cent.at[:, pl.ds(pl.multiple_of(zz * 128, 128), 128)], tb.at[8 - k, c], sub=zz * 2 + c)
    with jax.named_scope("zwait"):
        drain(zbuf, rcv.at[ZFAR])
    with jax.named_scope("tabsend"):
        tb[3:6, c, rows16] = zbuf[...]
        for j in range(1, 16):
            send(TAB, zbuf, tb.at[3:6, c, rows16], dp=(dp + j) % 16)
    with jax.named_scope("finwait"):
        drain(mz.at[0:7], rcv.at[OVERZ])
    with jax.named_scope("merge2"):
        mv = mz[:, 0:12, :]
        big = jnp.max(mv, axis=0)
        fs[c, 0:12, :] = big
        fs[c, 12:24, :] = jnp.sum(mz[:, 12:24, :] * jnp.exp(mv - big[None]), axis=0)
        send(BACK, fs.at[c], fs.at[c], sub=other)
        drain(ra, rcv.at[BACK])
    with jax.named_scope("weights"):
        cp_ = jnp.zeros((KL, 128), F32)
        for h in range(2):
            scl[h] = jnp.exp(st[h, 0:12, :] - fs[h, 0:12, :]) / fs[h, 12:24, :]
        for k in range(NC):
            scale = []
            for i in range(RC // 128):
                h, r = divmod(k * (RC // 128) + i, 12)
                scale.append(scl[h, r:r + 1, :])
            p = eT[:, k * RC:(k + 1) * RC] * jnp.concatenate(scale, axis=1)
            for i in range(RC // 128):
                cp_ = cp_ + p[:, i * 128:(i + 1) * 128]
            wT[:, k * RC:(k + 1) * RC] = p.astype(BF16)
    def along(i, first, k):
        if (i == 0) == first:
            return y * 4 + (x + k) % 4, (x + k) % 4
        return ((y + k) % 4) * 4 + x, (y + k) % 4

    ax = [(x, y), (y, x)]
    with jax.named_scope("sums"):
        for h in range(2):
            for q in (2 * h, 2 * h + 1):
                sums[q] = jnp.dot(wT[...], emb[:, q * 256:(q + 1) * 256], preferred_element_type=F32)
            for k in (1, 3, 2):
                for i in range(2):
                    dev, pa = along(i, True, k)
                    send(CENT + h, sums.at[2 * h + i, pl.ds(pl.multiple_of(pa * 64, 64), 64), :],
                         r1.at[h, i, k - 1], dp=dev)
    with jax.named_scope("counts"):
        cg[dp] = jnp.broadcast_to(jnp.sum(jnp.transpose(cp_), axis=0, keepdims=True), (8, 256))
        for k in range(1, 16):
            send(COUNT, cg.at[dp], cg.at[dp], dp=(dp + k) % 16)

    with jax.named_scope("nearwait"):
        drain(tb.at[0:4, 0], rcv.at[ZNEAR])
        send(SWAP, tb.at[0:3, c], tb.at[0:3, c], sub=other)
        send(SWAP, tb.at[6:8, c], tb.at[6:8, c], sub=other)
    with jax.named_scope("tabwait"):
        drain(tb.at[3:6, 0, 0:240], rcv.at[TAB])
        send(SWAP2, tb.at[3:6, c], tb.at[3:6, c], sub=other)
    with jax.named_scope("swap"):
        drain(tb.at[0:5, 0], rcv.at[SWAP])
        drain(tb.at[0:3, 0], rcv.at[SWAP2])
        la.wait()
    with jax.named_scope("widen"):
        for i in range(8):
            for j in range(2):
                at = pl.multiple_of(((z + i) % 8) * 512 + j * 256, 256)
                tf[pl.ds(at, 256), :] = tb[i, j].astype(F32)
    with jax.named_scope("gather"):
        def fetch(i, _):
            o = pl.multiple_of(i * 32, 32)
            for j in range(32):
                xg[pl.ds(o + j, 1), :] = tf[pl.ds(asg[o + j], 1), :]
            return 0
        lax.fori_loop(0, R // 32, fetch, 0)
    with jax.named_scope("turn"):
        mine = (lax.broadcasted_iota(jnp.int32, (RC, 128), 1) // 64) == c
        for k in range(NC):
            g = xg[pl.ds(k * RC, RC), :]
            cenT[:, pl.ds(k * RC, RC)] = jnp.transpose(g).astype(BF16)
            xgb[pl.ds(k * RC, RC), :] = jnp.where(mine, g, 1.0).astype(BF16)

    def stage1(h):
        drain(r1.at[h], rcv.at[CENT + h])
        for i in range(2):
            q = 2 * h + i
            s1[q] = (sums[q, pl.ds(pl.multiple_of(ax[i][0] * 64, 64), 64), :]
                     + r1[h, i, 0] + r1[h, i, 1] + r1[h, i, 2])
        for k in (1, 3, 2):
            for i in range(2):
                dev, pb = along(i, False, k)
                send(CENT + 2 + h, s1.at[2 * h + i, pl.ds(pl.multiple_of(pb * 16, 16), 16), :],
                     r2.at[h, i, k - 1], dp=dev)

    def stage2(h):
        drain(r2.at[h], rcv.at[CENT + 2 + h])
        for i in range(2):
            q = 2 * h + i
            a, b = ax[i]
            row = pl.ds(pl.multiple_of(a * 64 + b * 16, 16), 16)
            qs = slice(q * 256, (q + 1) * 256)
            fin = s1[q, pl.ds(pl.multiple_of(b * 16, 16), 16), :] + r2[h, i, 0] + r2[h, i, 1] + r2[h, i, 2]
            den = cc[row, :]
            out_ref[row, qs] = (fin + cent[row, qs].astype(F32)) / jnp.concatenate([den, den], axis=1)
        for k in (1, 3, 2):
            for i in range(2):
                a, b = ax[i]
                piece = out_ref.at[pl.ds(pl.multiple_of(a * 64 + b * 16, 16), 16), pl.ds((2 * h + i) * 256, 256)]
                send(CENT + 4 + h, piece, piece, dp=along(i, False, k)[0])

    def stage3(h):
        drain(r2.at[h], rcv.at[CENT + 4 + h])
        for k in (1, 3, 2):
            for i in range(2):
                piece = out_ref.at[pl.ds(pl.multiple_of(ax[i][0] * 64, 64), 64), pl.ds((2 * h + i) * 256, 256)]
                send(CENT + 6 + h, piece, piece, dp=along(i, True, k)[0])

    one = jnp.ones((16, RC), BF16)

    def code_logits(i):
        k, s = i // 4, i % 4
        cols = pl.ds(k * RC, RC)
        f = pl.ds(pl.multiple_of(c * 64 + 16 * s, 16), 16)
        es, cs_ = embT[f, cols], cenT[f, cols]
        xt = jnp.concatenate([es, es, es, cs_, cs_, cs_, one, one], axis=0)
        lsc[i % 2] = jnp.dot(cbt[s], xt, preferred_element_type=F32)

    def code(lo_, hi_):
        for i in range(lo_, hi_):
            k, s = i // 4, i % 4
            if i + 1 < 4 * NC:
                code_logits(i + 1)
            for j in range(RC // 256):
                l = lsc[i % 2, :, j * 256:(j + 1) * 256]
                e = jnp.exp2(l - jnp.max(l, axis=0, keepdims=True))
                w = e * (1.0 / jnp.sum(e, axis=0, keepdims=True))
                hi = w.astype(BF16)
                wh[s, :, j * 256:(j + 1) * 256] = hi
                wh[s, :, RC + j * 256:RC + (j + 1) * 256] = (w - hi.astype(F32)).astype(BF16)
            rows = pl.ds(k * RC, RC)
            both = jnp.concatenate([emb[rows, lanes128], xgb[rows, :]], axis=1)
            acc[s] += (jnp.dot(wh[s, :, 0:RC], both, preferred_element_type=F32)
                       + jnp.dot(wh[s, :, RC:2 * RC], both, preferred_element_type=F32))

    with jax.named_scope("code1"):
        code_logits(0)
        code(0, 4)
    with jax.named_scope("s1A"):
        stage1(0)
    with jax.named_scope("code2"):
        code(4, 12)
    with jax.named_scope("s1B"):
        stage1(1)
    with jax.named_scope("code3"):
        code(12, 16)
    with jax.named_scope("cntwait"):
        drain(cg.at[0:15], rcv.at[COUNT])
        ctot = jnp.sum(cg[...], axis=0)[0:1]
        cc[...] = jnp.transpose(jnp.broadcast_to(ctot, (128, 256))) + 1.0
    with jax.named_scope("s2A"):
        stage2(0)
    with jax.named_scope("code4"):
        code(16, 4 * NC)
    with jax.named_scope("codeprep"):
        for s in range(4):
            accT[...] = jnp.transpose(acc[s])
            f = pl.multiple_of(c * 64 + s * 16, 16)
            tot16 = accT[pl.ds(f, 16), :] - accT[pl.ds(pl.multiple_of(128 + f, 16), 16), :]
            cnt = accT[pl.ds(pl.multiple_of(128 + (1 - c) * 64, 64), 8), :]
            for h in range(2):
                for g in range(2):
                    cs[s * 4 + h * 2 + g, 0:8, :] = tot16[8 * g:8 * g + 8, 128 * h:128 * h + 128]
                    cs[s * 4 + h * 2 + g, 8:16, :] = cnt[:, 128 * h:128 * h + 128]
        for k in range(1, 16):
            o = (dp + k) % 16
            send(CODE, cs.at[o], cr.at[dp], dp=o)
        cr[dp] = cs[dp]
    with jax.named_scope("s2B"):
        stage2(1)
    with jax.named_scope("s3A"):
        stage3(0)
    with jax.named_scope("s3B"):
        stage3(1)
    with jax.named_scope("codewait"):
        drain(cr.at[0:15], rcv.at[CODE])
    with jax.named_scope("codefin"):
        t = jnp.sum(cr[...], axis=0)
        so, ho, go = dp // 4, (dp // 2) % 2, dp % 2
        g8 = pl.ds(pl.multiple_of(go * 8, 8), 8)
        h128 = pl.ds(pl.multiple_of(ho * 128, 128), 128)
        cbo_ref[so, g8, h128] = (t[0:8] + cb[so, g8, h128]) / (t[8:16] + 1.0)
        for k in range(1, 16):
            piece = cbo_ref.at[so, g8, h128]
            send(NEWCODE, piece, piece, dp=(dp + k) % 16)
    with jax.named_scope("newcent"):
        drain(r1.at[0], rcv.at[CENT + 6])
        drain(r1.at[1], rcv.at[CENT + 7])
    with jax.named_scope("newcode"):
        drain(cr.at[0:15, 0:8], rcv.at[NEWCODE])
    with jax.named_scope("sent"):
        sizes = {
            PAIR: ra, BACK: ra, ZFAR: zbuf, ZNEAR: tb.at[0:4, 0], TAB: tb.at[3:6, 0, 0:240], SWAP: tb.at[0:5, 0],
            SWAP2: tb.at[0:3, 0], OVERZ: mz.at[0:7], COUNT: cg.at[0:15], CODE: cr.at[0:15], NEWCODE: cr.at[0:15, 0:8],
        }
        for h in range(2):
            sizes |= {CENT + h: r1.at[h], CENT + 2 + h: r2.at[h], CENT + 4 + h: r2.at[h], CENT + 6 + h: r1.at[h]}
        for phase, ref in sizes.items():
            drain(ref, snd.at[phase])


def shards(embeddings, assignment, centroids, codebooks):
    dma = pltpu.SemaphoreType.DMA
    v = pltpu.VMEM
    hbm = pl.BlockSpec(memory_space=pltpu.HBM)
    vm = pl.BlockSpec(memory_space=pltpu.VMEM)
    return pl.pallas_call(
        kernel,
        out_shape=(v((KL, D), F32), v((4, 16, 256), F32)),
        in_specs=[hbm] * 4,
        out_specs=(vm, vm),
        scratch_shapes=[
            v((R, D), BF16), pltpu.SMEM((R,), jnp.int32), v((KL, D), BF16), v((4, 16, 256), F32),
            v((KL, R), F32), v((KL, R), BF16),
            v((2, 24, 128), F32), v((24, 128), F32), v((8, 24, 128), F32), v((2, 24, 128), F32), v((2, 12, 128), F32),
            v((3, 16, 128), BF16), v((8, 2, 256, 128), BF16), v((4096, 128), F32), v((R, 128), F32),
            v((128, R), BF16), v((128, R), BF16), v((4, 256, 128), BF16),
            v((4, 256, 256), F32), v((2, 2, 3, 64, 256), F32), v((4, 64, 256), F32), v((2, 2, 3, 16, 256), F32),
            v((16, 8, 256), F32), v((256, 128), F32), v((4, 256, 256), F32), v((256, 256), F32),
            v((16, 16, 128), F32), v((16, 16, 128), F32),
            v((R, 128), BF16), v((2, 256, RC), F32), v((4, 256, 2 * RC), BF16),
            dma((6,)), dma((PHASES,)), dma((PHASES,)),
        ],
        compiler_params=pltpu.CompilerParams(
            collective_id=0, has_side_effects=True, vmem_limit_bytes=60 * 1024 * 1024),
        name="step",
    )(*(pltpu.with_memory_space_constraint(a, pltpu.HBM) for a in (embeddings, assignment, centroids, codebooks)))


def solution(mesh):
    placed = (P("dp", None), P("dp"), P("sub", None), P("sub", None, None))
    return jax.shard_map(
        shards,
        mesh=mesh,
        in_specs=placed,
        out_specs=(P("sub", None), P("sub", None, None)),
        check_vma=False,
    )
```

```python
import jax
import jax.numpy as jnp
from jax import lax
from jax.experimental import pallas as pl
from jax.experimental.pallas import tpu as pltpu
from jax.sharding import PartitionSpec as P

R, D, KL = 3072, 1024, 256
NC, RC = 6, 512
PAIR, BACK, ZFAR, ZNEAR, ZNEAR2, TAB, SWAP, SWAP2, SWAP3, BASE, OVERZ, COUNT, CODE, NEWCODE, CENT = range(15)
PHASES = CENT + 8
F32, BF16 = jnp.float32, jnp.bfloat16
LOG2E = 1.4426950408889634


def rcopy(src, dst, ssem, rsem, **where):
    return pltpu.make_async_remote_copy(
        src_ref=src, dst_ref=dst, send_sem=ssem, recv_sem=rsem,
        device_id=where, device_id_type=pl.DeviceIdType.MESH,
    )


def drain(ref, sem):
    pltpu.make_async_copy(ref, ref, sem).wait()


def split3(v):
    a = v.astype(BF16).astype(F32)
    r = v - a
    b = r.astype(BF16).astype(F32)
    return a, b, (r - b).astype(BF16).astype(F32)


def kernel(
    emb_hbm, asg_hbm, cent_hbm, cb_hbm, out_ref, cbo_ref,
    emb, asg, cent, cb, eT, wT, ml, st, ra, mz, fs, scl, zbuf, tb, tf, xg, gb, embT, cenT, cbt,
    sums, r1, s1, r2, cg, cc, acc, accT, cs, cr, xgb, lsc, wh,
    lsem, snd, rcv,
):
    dp = lax.axis_index("dp")
    sub = lax.axis_index("sub")
    y, x = dp // 4, dp % 4
    z, c = sub // 2, sub % 2

    def send(phase, src, dst, **where):
        rcopy(src, dst, snd.at[phase], rcv.at[phase], **where).start()

    with jax.named_scope("load"):
        lc = pltpu.make_async_copy(cent_hbm, cent, lsem.at[3])
        lb = pltpu.make_async_copy(cb_hbm, cb, lsem.at[4])
        la = pltpu.make_async_copy(asg_hbm, asg, lsem.at[5])
        lc.start()
        loads = []
        for k in range(3):
            sl = pl.ds(k * 1024, 1024)
            cp = pltpu.make_async_copy(emb_hbm.at[sl, :], emb.at[sl, :], lsem.at[k])
            cp.start()
            loads.append(cp)
        lb.start()
        la.start()
        bar = pltpu.get_barrier_semaphore()
        for k in range(1, 16):
            pl.semaphore_signal(bar, inc=1, device_id={"sub": (sub + k) % 16}, device_id_type=pl.DeviceIdType.MESH)
            pl.semaphore_signal(bar, inc=1, device_id={"dp": (dp + k) % 16}, device_id_type=pl.DeviceIdType.MESH)
        acc[...] = jnp.zeros(acc.shape, F32)
        st[...] = jnp.zeros(st.shape, F32)
        ml[...] = jnp.zeros(ml.shape, F32)
        rows16 = pl.ds(pl.multiple_of(dp * 16, 16), 16)
        lanes128 = pl.ds(pl.multiple_of(z * 128, 128), 128)
        lc.wait()
        tb[0, c] = cent[:, lanes128]

    with jax.named_scope("logits"):
        pad_one = jnp.where(lax.broadcasted_iota(jnp.int32, (2, 16, 128), 1) < 12, 0.0, 1.0)
        cf = cent[...].astype(F32)
        hn = 0.5 * jnp.sum(cf * cf, axis=1, keepdims=True)
        for k in range(NC):
            if k % 2 == 0:
                loads[k // 2].wait()
            l = lax.dot_general(cent[...], emb[k * RC:(k + 1) * RC, :], (((1,), (1,)), ((), ())),
                                preferred_element_type=F32) - hn
            m = jnp.max(l, axis=0, keepdims=True)
            e = jnp.exp(l - m)
            s = jnp.sum(e, axis=0, keepdims=True)
            eT[:, k * RC:(k + 1) * RC] = e
            for i in range(RC // 128):
                h, r = divmod(k * (RC // 128) + i, 12)
                ml[h, r:r + 1, :] = m[:, i * 128:(i + 1) * 128]
                st[h, r:r + 1, :] = s[:, i * 128:(i + 1) * 128]
        st[...] = ml[...] + jnp.log(st[...] + pad_one)

    with jax.named_scope("barrier"):
        pl.semaphore_wait(bar, 30)
    with jax.named_scope("statsend"):
        other = z * 2 + (1 - c)
        send(PAIR, st.at[1 - c], ra, sub=other)
    with jax.named_scope("zsend"):
        for k in range(3, 6):
            zz = (z + k) % 8
            send(ZFAR, cent.at[rows16, pl.ds(pl.multiple_of(zz * 128, 128), 128)], zbuf.at[5 - k], sub=zz * 2 + c)
    with jax.named_scope("cbprep"):
        lb.wait()
        for s in range(4):
            v = cb[s]
            parts = split3(v * LOG2E)
            half = split3(-0.5 * LOG2E * jnp.sum(v * v, axis=0, keepdims=True))
            neg = tuple(-p for p in parts)
            stack = jnp.concatenate(parts + neg + half + (jnp.zeros((29, 256), F32),), axis=0)
            cbt[s] = jnp.transpose(stack).astype(BF16)
        for k in range(NC):
            o = k * RC
            embT[:, pl.ds(o, RC)] = jnp.transpose(emb[pl.ds(o, RC), lanes128].astype(F32)).astype(BF16)

    with jax.named_scope("statwait"):
        drain(ra, rcv.at[PAIR])
    with jax.named_scope("merge"):
        ma, mb = st[c], ra[...]
        big = jnp.maximum(ma, mb)
        mz[z] = big + jnp.log(jnp.exp(ma - big) + jnp.exp(mb - big))
        for k in range(1, 8):
            send(OVERZ, mz.at[z], mz.at[z], sub=((z + k) % 8) * 2 + c)
        for k in (1, 7, 2, 6):
            zz = (z + k) % 8
            send(ZNEAR if k in (1, 7) else ZNEAR2, cent.at[:, pl.ds(pl.multiple_of(zz * 128, 128), 128)], tb.at[8 - k, c], sub=zz * 2 + c)
    with jax.named_scope("zwait"):
        drain(zbuf, rcv.at[ZFAR])
    with jax.named_scope("tabsend"):
        tb[3:6, c, rows16] = zbuf[...]
        for j in range(1, 16):
            send(TAB, zbuf, tb.at[3:6, c, rows16], dp=(dp + j) % 16)
    with jax.named_scope("finwait"):
        drain(mz.at[0:7], rcv.at[OVERZ])
    with jax.named_scope("merge2"):
        mv = mz[...]
        big = jnp.max(mv, axis=0)
        fs[c] = big + jnp.log(jnp.sum(jnp.exp(mv - big[None]), axis=0))
        send(BACK, fs.at[c], fs.at[c], sub=other)
        drain(tb.at[0:2, 0], rcv.at[ZNEAR])
        send(SWAP, tb.at[0:2, c], tb.at[0:2, c], sub=other)
        send(SWAP, tb.at[7, c], tb.at[7, c], sub=other)
        drain(ra, rcv.at[BACK])
    with jax.named_scope("weights"):
        cp_ = jnp.zeros((KL, 128), F32)
        for h in range(2):
            scl[h] = jnp.exp(ml[h] - fs[h])
        for k in range(NC):
            scale = []
            for i in range(RC // 128):
                h, r = divmod(k * (RC // 128) + i, 12)
                scale.append(scl[h, r:r + 1, :])
            p = eT[:, k * RC:(k + 1) * RC] * jnp.concatenate(scale, axis=1)
            for i in range(RC // 128):
                cp_ = cp_ + p[:, i * 128:(i + 1) * 128]
            wT[:, k * RC:(k + 1) * RC] = p.astype(BF16)
    def along(i, first, k):
        if (i == 0) == first:
            return y * 4 + (x + k) % 4, (x + k) % 4
        return ((y + k) % 4) * 4 + x, (y + k) % 4

    ax = [(x, y), (y, x)]
    with jax.named_scope("sums"):
        for h in range(2):
            for q in (2 * h, 2 * h + 1):
                sums[q] = jnp.dot(wT[...], emb[:, q * 256:(q + 1) * 256], preferred_element_type=F32)
            for k in (1, 3, 2):
                for i in range(2):
                    dev, pa = along(i, True, k)
                    send(CENT + h, sums.at[2 * h + i, pl.ds(pl.multiple_of(pa * 64, 64), 64), :],
                         r1.at[h, i, k - 1], dp=dev)
    with jax.named_scope("counts"):
        cg[dp] = jnp.broadcast_to(jnp.sum(jnp.transpose(cp_), axis=0, keepdims=True), (8, 256))
        for k in range(1, 16):
            send(COUNT, cg.at[dp], cg.at[dp], dp=(dp + k) % 16)

    with jax.named_scope("nearwait"):
        drain(tb.at[0:2, 0], rcv.at[ZNEAR2])
        send(SWAP2, tb.at[2, c], tb.at[2, c], sub=other)
        send(SWAP2, tb.at[6, c], tb.at[6, c], sub=other)
    with jax.named_scope("tabwait"):
        drain(tb.at[3:6, 0, 0:240], rcv.at[TAB])
        send(SWAP3, tb.at[3:6, c], tb.at[3:6, c], sub=other)
    with jax.named_scope("swap"):
        drain(tb.at[0:3, 0], rcv.at[SWAP])
        drain(tb.at[0:2, 0], rcv.at[SWAP2])
        drain(tb.at[0:3, 0], rcv.at[SWAP3])
        la.wait()
    with jax.named_scope("widen"):
        for i in range(8):
            for j in range(2):
                at = pl.multiple_of(((z + i) % 8) * 512 + j * 256, 256)
                tf[pl.ds(at, 256), :] = tb[i, j].astype(F32)
    with jax.named_scope("gather"):
        def fetch(i, _):
            o = pl.multiple_of(i * 32, 32)
            for j in range(32):
                xg[pl.ds(o + j, 1), :] = tf[pl.ds(asg[first + o + j], 1), :]
            return 0
        first = c * (R // 2)
        for k in range(3):
            lax.fori_loop(k * 16, (k + 1) * 16, fetch, 0)
            part = pl.ds(k * RC, RC)
            gb[c, part, :] = xg[part, :].astype(BF16)
            send(BASE, gb.at[c, part], gb.at[c, part], sub=other)

    def block(k):
        return pl.ds(pl.multiple_of(((c + k // 3) % 2 * 3 + k % 3) * RC, RC), RC)

    mine = (lax.broadcasted_iota(jnp.int32, (RC, 128), 1) // 64) == c

    def turn(k):
        g = gb[(c + k // 3) % 2, pl.ds(k % 3 * RC, RC), :].astype(F32)
        cenT[:, block(k)] = jnp.transpose(g).astype(BF16)
        xgb[block(k), :] = jnp.where(mine, g, 1.0).astype(BF16)

    def stage1(h):
        drain(r1.at[h], rcv.at[CENT + h])
        for i in range(2):
            q = 2 * h + i
            s1[q] = (sums[q, pl.ds(pl.multiple_of(ax[i][0] * 64, 64), 64), :]
                     + r1[h, i, 0] + r1[h, i, 1] + r1[h, i, 2])
        for k in (1, 3, 2):
            for i in range(2):
                dev, pb = along(i, False, k)
                send(CENT + 2 + h, s1.at[2 * h + i, pl.ds(pl.multiple_of(pb * 16, 16), 16), :],
                     r2.at[h, i, k - 1], dp=dev)

    def stage2(h):
        drain(r2.at[h], rcv.at[CENT + 2 + h])
        for i in range(2):
            q = 2 * h + i
            a, b = ax[i]
            row = pl.ds(pl.multiple_of(a * 64 + b * 16, 16), 16)
            qs = slice(q * 256, (q + 1) * 256)
            fin = s1[q, pl.ds(pl.multiple_of(b * 16, 16), 16), :] + r2[h, i, 0] + r2[h, i, 1] + r2[h, i, 2]
            den = cc[row, :]
            out_ref[row, qs] = (fin + cent[row, qs].astype(F32)) / jnp.concatenate([den, den], axis=1)
        for k in (1, 3, 2):
            for i in range(2):
                a, b = ax[i]
                piece = out_ref.at[pl.ds(pl.multiple_of(a * 64 + b * 16, 16), 16), pl.ds((2 * h + i) * 256, 256)]
                send(CENT + 4 + h, piece, piece, dp=along(i, False, k)[0])

    def stage3(h):
        drain(r2.at[h], rcv.at[CENT + 4 + h])
        for k in (1, 3, 2):
            for i in range(2):
                piece = out_ref.at[pl.ds(pl.multiple_of(ax[i][0] * 64, 64), 64), pl.ds((2 * h + i) * 256, 256)]
                send(CENT + 6 + h, piece, piece, dp=along(i, True, k)[0])

    one = jnp.ones((16, RC), BF16)

    def code_logits(i):
        k, s = i // 4, i % 4
        cols = block(k)
        f = pl.ds(pl.multiple_of(c * 64 + 16 * s, 16), 16)
        es, cs_ = embT[f, cols], cenT[f, cols]
        xt = jnp.concatenate([es, es, es, cs_, cs_, cs_, one, one], axis=0)
        lsc[i % 2] = jnp.dot(cbt[s], xt, preferred_element_type=F32)

    def code(lo_, hi_):
        for i in range(lo_, hi_):
            k, s = i // 4, i % 4
            if i + 1 < 4 * NC:
                code_logits(i + 1)
            for j in range(RC // 256):
                l = lsc[i % 2, :, j * 256:(j + 1) * 256]
                e = jnp.exp2(l - jnp.max(l, axis=0, keepdims=True))
                w = e * (1.0 / jnp.sum(e, axis=0, keepdims=True))
                hi = w.astype(BF16)
                wh[s, :, j * 256:(j + 1) * 256] = hi
                wh[s, :, RC + j * 256:RC + (j + 1) * 256] = (w - hi.astype(F32)).astype(BF16)
            rows = block(k)
            both = jnp.concatenate([emb[rows, lanes128], xgb[rows, :]], axis=1)
            acc[s] += (jnp.dot(wh[s, :, 0:RC], both, preferred_element_type=F32)
                       + jnp.dot(wh[s, :, RC:2 * RC], both, preferred_element_type=F32))

    with jax.named_scope("code1"):
        for k in range(3):
            turn(k)
        code_logits(0)
        code(0, 8)
    with jax.named_scope("s1A"):
        stage1(0)
    with jax.named_scope("code2"):
        code(8, 11)
        drain(gb.at[0], rcv.at[BASE])
        for k in range(3, 6):
            turn(k)
        code(11, 16)
    with jax.named_scope("s1B"):
        stage1(1)
    with jax.named_scope("code3"):
        code(16, 20)
    with jax.named_scope("cntwait"):
        drain(cg.at[0:15], rcv.at[COUNT])
        ctot = jnp.sum(cg[...], axis=0)[0:1]
        cc[...] = jnp.transpose(jnp.broadcast_to(ctot, (128, 256))) + 1.0
    with jax.named_scope("s2A"):
        stage2(0)
    with jax.named_scope("code4"):
        code(20, 4 * NC)
    with jax.named_scope("codeprep"):
        for s in range(4):
            accT[...] = jnp.transpose(acc[s])
            f = pl.multiple_of(c * 64 + s * 16, 16)
            tot16 = accT[pl.ds(f, 16), :] - accT[pl.ds(pl.multiple_of(128 + f, 16), 16), :]
            cnt = accT[pl.ds(pl.multiple_of(128 + (1 - c) * 64, 64), 8), :]
            for h in range(2):
                for g in range(2):
                    cs[s * 4 + h * 2 + g, 0:8, :] = tot16[8 * g:8 * g + 8, 128 * h:128 * h + 128]
                    cs[s * 4 + h * 2 + g, 8:16, :] = cnt[:, 128 * h:128 * h + 128]
        for k in range(1, 16):
            o = (dp + k) % 16
            send(CODE, cs.at[o], cr.at[dp], dp=o)
        cr[dp] = cs[dp]
    with jax.named_scope("s2B"):
        stage2(1)
    with jax.named_scope("s3A"):
        stage3(0)
    with jax.named_scope("s3B"):
        stage3(1)
    with jax.named_scope("codewait"):
        drain(cr.at[0:15], rcv.at[CODE])
    with jax.named_scope("codefin"):
        t = jnp.sum(cr[...], axis=0)
        so, ho, go = dp // 4, (dp // 2) % 2, dp % 2
        g8 = pl.ds(pl.multiple_of(go * 8, 8), 8)
        h128 = pl.ds(pl.multiple_of(ho * 128, 128), 128)
        cbo_ref[so, g8, h128] = (t[0:8] + cb[so, g8, h128]) / (t[8:16] + 1.0)
        for k in range(1, 16):
            piece = cbo_ref.at[so, g8, h128]
            send(NEWCODE, piece, piece, dp=(dp + k) % 16)
    with jax.named_scope("newcent"):
        drain(r1.at[0], rcv.at[CENT + 6])
        drain(r1.at[1], rcv.at[CENT + 7])
    with jax.named_scope("newcode"):
        drain(cr.at[0:15, 0:8], rcv.at[NEWCODE])
    with jax.named_scope("sent"):
        sizes = {
            PAIR: ra, BACK: ra, ZFAR: zbuf, ZNEAR: tb.at[0:2, 0], ZNEAR2: tb.at[0:2, 0],
            TAB: tb.at[3:6, 0, 0:240], SWAP: tb.at[0:3, 0], SWAP2: tb.at[0:2, 0], SWAP3: tb.at[0:3, 0],
            BASE: gb.at[0], OVERZ: mz.at[0:7], COUNT: cg.at[0:15], CODE: cr.at[0:15], NEWCODE: cr.at[0:15, 0:8],
        }
        for h in range(2):
            sizes |= {CENT + h: r1.at[h], CENT + 2 + h: r2.at[h], CENT + 4 + h: r2.at[h], CENT + 6 + h: r1.at[h]}
        for phase, ref in sizes.items():
            drain(ref, snd.at[phase])


def unload(cent_vm, code_vm, cent_out, code_out, sem):
    a = pltpu.make_async_copy(cent_vm, cent_out, sem.at[0])
    b = pltpu.make_async_copy(code_vm, code_out, sem.at[1])
    a.start()
    b.start()
    a.wait()
    b.wait()


def shards(embeddings, assignment, centroids, codebooks):
    dma = pltpu.SemaphoreType.DMA
    v = pltpu.VMEM
    hbm = pl.BlockSpec(memory_space=pltpu.HBM)
    vm = pl.BlockSpec(memory_space=pltpu.VMEM)
    outs = pl.pallas_call(
        kernel,
        out_shape=(v((KL, D), F32), v((4, 16, 256), F32)),
        in_specs=[hbm] * 4,
        out_specs=(vm, vm),
        scratch_shapes=[
            v((R, D), BF16), pltpu.SMEM((R,), jnp.int32), v((KL, D), BF16), v((4, 16, 256), F32),
            v((KL, R), F32), v((KL, R), BF16),
            v((2, 16, 128), F32), v((2, 16, 128), F32), v((16, 128), F32), v((8, 16, 128), F32), v((2, 16, 128), F32),
            v((2, 16, 128), F32),
            v((3, 16, 128), BF16), v((8, 2, 256, 128), BF16), v((4096, 128), F32), v((R // 2, 128), F32), v((2, R // 2, 128), BF16),
            v((128, R), BF16), v((128, R), BF16), v((4, 256, 128), BF16),
            v((4, 256, 256), F32), v((2, 2, 3, 64, 256), F32), v((4, 64, 256), F32), v((2, 2, 3, 16, 256), F32),
            v((16, 8, 256), F32), v((256, 128), F32), v((4, 256, 256), F32), v((256, 256), F32),
            v((16, 16, 128), F32), v((16, 16, 128), F32),
            v((R, 128), BF16), v((2, 256, RC), F32), v((4, 256, 2 * RC), BF16),
            dma((6,)), dma((PHASES,)), dma((PHASES,)),
        ],
        compiler_params=pltpu.CompilerParams(
            collective_id=0, has_side_effects=True, vmem_limit_bytes=60 * 1024 * 1024),
        name="step",
    )(*(pltpu.with_memory_space_constraint(a, pltpu.HBM) for a in (embeddings, assignment, centroids, codebooks)))
    hb = pltpu.HBM
    return pl.pallas_call(
        unload,
        out_shape=(hb((KL, D), F32), hb((4, 16, 256), F32)),
        in_specs=[vm] * 2,
        out_specs=(hbm, hbm),
        scratch_shapes=[dma((2,))],
        name="unload",
    )(*(pltpu.with_memory_space_constraint(a, pltpu.VMEM) for a in outs))


def solution(mesh):
    placed = (P("dp", None), P("dp"), P("sub", None), P("sub", None, None))
    return jax.shard_map(
        shards,
        mesh=mesh,
        in_specs=placed,
        out_specs=(P("sub", None), P("sub", None, None)),
        check_vma=False,
    )
```

```python
import jax
import jax.numpy as jnp
from jax import lax
from jax.experimental import pallas as pl
from jax.experimental.pallas import tpu as pltpu
from jax.sharding import PartitionSpec as P

R, D, KL = 3072, 1024, 256
NC, RC = 6, 512
LOADS = ((0, 512), (512, 1024), (1536, 1024), (2560, 512))
PAIR, BACK, ZFAR, ZNEAR, ZNEAR2, TAB, SWAP, SWAP2, SWAP3, BASE, OVERZ, COUNT, CODE, NEWCODE, CENT = range(15)
PHASES = CENT + 8
F32, BF16 = jnp.float32, jnp.bfloat16
LOG2E = 1.4426950408889634


def rcopy(src, dst, ssem, rsem, **where):
    return pltpu.make_async_remote_copy(
        src_ref=src, dst_ref=dst, send_sem=ssem, recv_sem=rsem,
        device_id=where, device_id_type=pl.DeviceIdType.MESH,
    )


def drain(ref, sem):
    pltpu.make_async_copy(ref, ref, sem).wait()


def split3(v):
    a = v.astype(BF16).astype(F32)
    r = v - a
    b = r.astype(BF16).astype(F32)
    return a, b, (r - b).astype(BF16).astype(F32)


def kernel(
    emb_hbm, asg_hbm, cent_hbm, cb_hbm, out_ref, cbo_ref,
    emb, asg, cent, cb, eT, wT, ml, st, ra, mz, fs, scl, zbuf, tb, tf, xg, gb, embT, cenT, cbt,
    sums, r1, s1, r2, cg, cc, acc, accT, cs, cr, xgb, lsc, wh,
    lsem, snd, rcv,
):
    dp = lax.axis_index("dp")
    sub = lax.axis_index("sub")
    y, x = dp // 4, dp % 4
    z, c = sub // 2, sub % 2

    def send(phase, src, dst, **where):
        rcopy(src, dst, snd.at[phase], rcv.at[phase], **where).start()

    with jax.named_scope("load"):
        lc = pltpu.make_async_copy(cent_hbm, cent, lsem.at[0])
        lb = pltpu.make_async_copy(cb_hbm, cb, lsem.at[1])
        la = pltpu.make_async_copy(asg_hbm, asg, lsem.at[2])
        lc.start()
        loads = {}
        for k, (r0, n) in enumerate(LOADS):
            cp = pltpu.make_async_copy(emb_hbm.at[r0:r0 + n, :], emb.at[r0:r0 + n, :], lsem.at[3 + k])
            cp.start()
            loads[r0 // RC] = cp
        bar = pltpu.get_barrier_semaphore()
        for k in range(1, 16):
            pl.semaphore_signal(bar, inc=1, device_id={"sub": (sub + k) % 16}, device_id_type=pl.DeviceIdType.MESH)
            pl.semaphore_signal(bar, inc=1, device_id={"dp": (dp + k) % 16}, device_id_type=pl.DeviceIdType.MESH)
        lb.start()
        la.start()
        st[...] = jnp.zeros(st.shape, F32)
        ml[...] = jnp.zeros(ml.shape, F32)
        rows16 = pl.ds(pl.multiple_of(dp * 16, 16), 16)
        lanes128 = pl.ds(pl.multiple_of(z * 128, 128), 128)

    with jax.named_scope("logits"):
        pad_one = jnp.where(lax.broadcasted_iota(jnp.int32, (2, 16, 128), 1) < 12, 0.0, 1.0)
        lc.wait()
        cf = cent[...].astype(F32)
        hn = 0.5 * jnp.sum(cf * cf, axis=1, keepdims=True)
        for k in range(NC):
            if k in loads:
                loads[k].wait()
            l = lax.dot_general(cent[...], emb[k * RC:(k + 1) * RC, :], (((1,), (1,)), ((), ())),
                                preferred_element_type=F32) - hn
            m = jnp.max(l, axis=0, keepdims=True)
            e = jnp.exp(l - m)
            s = jnp.sum(e, axis=0, keepdims=True)
            eT[:, k * RC:(k + 1) * RC] = e
            for i in range(RC // 128):
                h, r = divmod(k * (RC // 128) + i, 12)
                ml[h, r:r + 1, :] = m[:, i * 128:(i + 1) * 128]
                st[h, r:r + 1, :] = s[:, i * 128:(i + 1) * 128]
        st[...] = ml[...] + jnp.log(st[...] + pad_one)

    with jax.named_scope("barrier"):
        pl.semaphore_wait(bar, 30)
    with jax.named_scope("statsend"):
        other = z * 2 + (1 - c)
        send(PAIR, st.at[1 - c], ra, sub=other)
    with jax.named_scope("zsend"):
        for k in range(3, 6):
            zz = (z + k) % 8
            send(ZFAR, cent.at[rows16, pl.ds(pl.multiple_of(zz * 128, 128), 128)], zbuf.at[5 - k], sub=zz * 2 + c)
    with jax.named_scope("cbprep"):
        acc[...] = jnp.zeros(acc.shape, F32)
        tb[0, c] = cent[:, lanes128]
        lb.wait()
        for s in range(4):
            v = cb[s]
            parts = split3(v * LOG2E)
            half = split3(-0.5 * LOG2E * jnp.sum(v * v, axis=0, keepdims=True))
            neg = tuple(-p for p in parts)
            stack = jnp.concatenate(parts + neg + half + (jnp.zeros((29, 256), F32),), axis=0)
            cbt[s] = jnp.transpose(stack).astype(BF16)
        for k in range(NC):
            o = k * RC
            embT[:, pl.ds(o, RC)] = jnp.transpose(emb[pl.ds(o, RC), lanes128].astype(F32)).astype(BF16)

    with jax.named_scope("statwait"):
        drain(ra, rcv.at[PAIR])
    with jax.named_scope("merge"):
        ma, mb = st[c], ra[...]
        big = jnp.maximum(ma, mb)
        mz[z] = big + jnp.log(jnp.exp(ma - big) + jnp.exp(mb - big))
        for k in range(1, 8):
            send(OVERZ, mz.at[z], mz.at[z], sub=((z + k) % 8) * 2 + c)
        for k in (1, 7, 2, 6):
            zz = (z + k) % 8
            send(ZNEAR if k in (1, 7) else ZNEAR2, cent.at[:, pl.ds(pl.multiple_of(zz * 128, 128), 128)], tb.at[8 - k, c], sub=zz * 2 + c)
    with jax.named_scope("zwait"):
        drain(zbuf, rcv.at[ZFAR])
    with jax.named_scope("tabsend"):
        tb[3:6, c, rows16] = zbuf[...]
        for j in range(1, 16):
            send(TAB, zbuf, tb.at[3:6, c, rows16], dp=(dp + j) % 16)
    with jax.named_scope("finwait"):
        drain(mz.at[0:7], rcv.at[OVERZ])
    with jax.named_scope("merge2"):
        mv = mz[...]
        big = jnp.max(mv, axis=0)
        fs[c] = big + jnp.log(jnp.sum(jnp.exp(mv - big[None]), axis=0))
        send(BACK, fs.at[c], fs.at[c], sub=other)
        drain(tb.at[0:2, 0], rcv.at[ZNEAR])
        send(SWAP, tb.at[0:2, c], tb.at[0:2, c], sub=other)
        send(SWAP, tb.at[7, c], tb.at[7, c], sub=other)
        drain(ra, rcv.at[BACK])
    with jax.named_scope("weights"):
        cp_ = jnp.zeros((KL, 128), F32)
        for h in range(2):
            scl[h] = jnp.exp(ml[h] - fs[h])
        for k in range(NC):
            scale = []
            for i in range(RC // 128):
                h, r = divmod(k * (RC // 128) + i, 12)
                scale.append(scl[h, r:r + 1, :])
            p = eT[:, k * RC:(k + 1) * RC] * jnp.concatenate(scale, axis=1)
            for i in range(RC // 128):
                cp_ = cp_ + p[:, i * 128:(i + 1) * 128]
            wT[:, k * RC:(k + 1) * RC] = p.astype(BF16)
    def along(i, first, k):
        if (i == 0) == first:
            return y * 4 + (x + k) % 4, (x + k) % 4
        return ((y + k) % 4) * 4 + x, (y + k) % 4

    ax = [(x, y), (y, x)]
    with jax.named_scope("sums"):
        for h in range(2):
            for q in (2 * h, 2 * h + 1):
                sums[q] = jnp.dot(wT[...], emb[:, q * 256:(q + 1) * 256], preferred_element_type=F32)
            for k in (1, 3, 2):
                for i in range(2):
                    dev, pa = along(i, True, k)
                    send(CENT + h, sums.at[2 * h + i, pl.ds(pl.multiple_of(pa * 64, 64), 64), :],
                         r1.at[h, i, k - 1], dp=dev)
    with jax.named_scope("counts"):
        cg[dp, 0:1, :] = jnp.sum(jnp.transpose(cp_), axis=0, keepdims=True)
        for k in range(1, 16):
            send(COUNT, cg.at[dp, 0:1], cg.at[dp, 0:1], dp=(dp + k) % 16)

    with jax.named_scope("nearwait"):
        drain(tb.at[0:2, 0], rcv.at[ZNEAR2])
        send(SWAP2, tb.at[2, c], tb.at[2, c], sub=other)
        send(SWAP2, tb.at[6, c], tb.at[6, c], sub=other)
    with jax.named_scope("tabwait"):
        drain(tb.at[3:6, 0, 0:240], rcv.at[TAB])
        send(SWAP3, tb.at[3:6, c], tb.at[3:6, c], sub=other)
    with jax.named_scope("swap"):
        drain(tb.at[0:3, 0], rcv.at[SWAP])
        drain(tb.at[0:2, 0], rcv.at[SWAP2])
        drain(tb.at[0:3, 0], rcv.at[SWAP3])
        la.wait()
    with jax.named_scope("widen"):
        for i in range(8):
            for j in range(2):
                at = pl.multiple_of(((z + i) % 8) * 512 + j * 256, 256)
                tf[pl.ds(at, 256), :] = tb[i, j].astype(F32)
    with jax.named_scope("gather"):
        def fetch(i, _):
            o = pl.multiple_of(i * 128, 128)
            for j in range(128):
                xg[pl.ds(o + j, 1), :] = tf[pl.ds(asg[first + o + j], 1), :]
            return 0
        first = c * (R // 2)
        for k in range(3):
            lax.fori_loop(k * 4, (k + 1) * 4, fetch, 0)
            part = pl.ds(k * RC, RC)
            gb[c, part, :] = xg[part, :].astype(BF16)
            send(BASE, gb.at[c, part], gb.at[c, part], sub=other)

    def block(k):
        return pl.ds(pl.multiple_of(((c + k // 3) % 2 * 3 + k % 3) * RC, RC), RC)

    mine = (lax.broadcasted_iota(jnp.int32, (RC, 128), 1) // 64) == c

    def turn(k):
        g = gb[(c + k // 3) % 2, pl.ds(k % 3 * RC, RC), :].astype(F32)
        cenT[:, block(k)] = jnp.transpose(g).astype(BF16)
        xgb[block(k), :] = jnp.where(mine, g, 1.0).astype(BF16)

    def stage1(h):
        drain(r1.at[h], rcv.at[CENT + h])
        for i in range(2):
            q = 2 * h + i
            s1[q] = (sums[q, pl.ds(pl.multiple_of(ax[i][0] * 64, 64), 64), :]
                     + r1[h, i, 0] + r1[h, i, 1] + r1[h, i, 2])
        for k in (1, 3, 2):
            for i in range(2):
                dev, pb = along(i, False, k)
                send(CENT + 2 + h, s1.at[2 * h + i, pl.ds(pl.multiple_of(pb * 16, 16), 16), :],
                     r2.at[h, i, k - 1], dp=dev)

    def stage2(h):
        drain(r2.at[h], rcv.at[CENT + 2 + h])
        for i in range(2):
            q = 2 * h + i
            a, b = ax[i]
            row = pl.ds(pl.multiple_of(a * 64 + b * 16, 16), 16)
            qs = slice(q * 256, (q + 1) * 256)
            fin = s1[q, pl.ds(pl.multiple_of(b * 16, 16), 16), :] + r2[h, i, 0] + r2[h, i, 1] + r2[h, i, 2]
            den = cc[row, :]
            out_ref[row, qs] = (fin + cent[row, qs].astype(F32)) / jnp.concatenate([den, den], axis=1)
        for k in (1, 3, 2):
            for i in range(2):
                a, b = ax[i]
                piece = out_ref.at[pl.ds(pl.multiple_of(a * 64 + b * 16, 16), 16), pl.ds((2 * h + i) * 256, 256)]
                send(CENT + 4 + h, piece, piece, dp=along(i, False, k)[0])

    def stage3(h):
        drain(r2.at[h], rcv.at[CENT + 4 + h])
        for k in (1, 3, 2):
            for i in range(2):
                piece = out_ref.at[pl.ds(pl.multiple_of(ax[i][0] * 64, 64), 64), pl.ds((2 * h + i) * 256, 256)]
                send(CENT + 6 + h, piece, piece, dp=along(i, True, k)[0])

    one = jnp.ones((16, RC), BF16)

    def code_logits(i):
        k, s = i // 4, i % 4
        cols = block(k)
        f = pl.ds(pl.multiple_of(c * 64 + 16 * s, 16), 16)
        es, cs_ = embT[f, cols], cenT[f, cols]
        xt = jnp.concatenate([es, es, es, cs_, cs_, cs_, one, one], axis=0)
        lsc[i % 2] = jnp.dot(cbt[s], xt, preferred_element_type=F32)

    def code(lo_, hi_):
        for i in range(lo_, hi_):
            k, s = i // 4, i % 4
            if i + 1 < 4 * NC:
                code_logits(i + 1)
            for j in range(RC // 256):
                l = lsc[i % 2, :, j * 256:(j + 1) * 256]
                e = jnp.exp2(l - jnp.max(l, axis=0, keepdims=True))
                w = e * (1.0 / jnp.sum(e, axis=0, keepdims=True))
                hi = w.astype(BF16)
                wh[s, :, j * 256:(j + 1) * 256] = hi
                wh[s, :, RC + j * 256:RC + (j + 1) * 256] = (w - hi.astype(F32)).astype(BF16)
            rows = block(k)
            both = jnp.concatenate([emb[rows, lanes128], xgb[rows, :]], axis=1)
            acc[s] += (jnp.dot(wh[s, :, 0:RC], both, preferred_element_type=F32)
                       + jnp.dot(wh[s, :, RC:2 * RC], both, preferred_element_type=F32))

    with jax.named_scope("code1"):
        for k in range(3):
            turn(k)
        code_logits(0)
        code(0, 4)
    with jax.named_scope("s1A"):
        stage1(0)
    with jax.named_scope("code2"):
        code(4, 11)
    with jax.named_scope("basewait"):
        drain(gb.at[0], rcv.at[BASE])
    with jax.named_scope("code3"):
        for k in range(3, 6):
            turn(k)
        code(11, 12)
    with jax.named_scope("s1B"):
        stage1(1)
    with jax.named_scope("code4"):
        code(12, 16)
    with jax.named_scope("cntwait"):
        drain(cg.at[0:15, 0:1], rcv.at[COUNT])
        ctot = jnp.sum(cg[:, 0:1, :], axis=0)
        cc[...] = jnp.transpose(jnp.broadcast_to(ctot, (128, 256))) + 1.0
    with jax.named_scope("s2A"):
        stage2(0)
    with jax.named_scope("code5"):
        code(16, 22)
    with jax.named_scope("s2B"):
        stage2(1)
    with jax.named_scope("code6"):
        code(22, 4 * NC)
    with jax.named_scope("codeprep"):
        for s in range(4):
            accT[...] = jnp.transpose(acc[s])
            f = pl.multiple_of(c * 64 + s * 16, 16)
            tot16 = accT[pl.ds(f, 16), :] - accT[pl.ds(pl.multiple_of(128 + f, 16), 16), :]
            cnt = accT[pl.ds(pl.multiple_of(128 + (1 - c) * 64, 64), 8), :]
            for h in range(2):
                for g in range(2):
                    cs[s * 4 + h * 2 + g, 0:8, :] = tot16[8 * g:8 * g + 8, 128 * h:128 * h + 128]
                    cs[s * 4 + h * 2 + g, 8:9, :] = cnt[0:1, 128 * h:128 * h + 128]
        for k in range(1, 16):
            o = (dp + k) % 16
            send(CODE, cs.at[o, 0:9], cr.at[dp, 0:9], dp=o)
        cr[dp, 0:9, :] = cs[dp, 0:9, :]
    with jax.named_scope("s3A"):
        stage3(0)
    with jax.named_scope("s3B"):
        stage3(1)
    with jax.named_scope("codewait"):
        drain(cr.at[0:15, 0:9], rcv.at[CODE])
    with jax.named_scope("codefin"):
        t = jnp.sum(cr[:, 0:8, :], axis=0)
        n = jnp.sum(cr[:, 8:9, :], axis=0)
        so, ho, go = dp // 4, (dp // 2) % 2, dp % 2
        g8 = pl.ds(pl.multiple_of(go * 8, 8), 8)
        h128 = pl.ds(pl.multiple_of(ho * 128, 128), 128)
        cbo_ref[so, g8, h128] = (t + cb[so, g8, h128]) / (n + 1.0)
        for k in range(1, 16):
            piece = cbo_ref.at[so, g8, h128]
            send(NEWCODE, piece, piece, dp=(dp + k) % 16)
    with jax.named_scope("newcent"):
        drain(r1.at[0], rcv.at[CENT + 6])
        drain(r1.at[1], rcv.at[CENT + 7])
    with jax.named_scope("newcode"):
        drain(cr.at[0:15, 0:8], rcv.at[NEWCODE])
    with jax.named_scope("sent"):
        sizes = {
            PAIR: ra, BACK: ra, ZFAR: zbuf, ZNEAR: tb.at[0:2, 0], ZNEAR2: tb.at[0:2, 0],
            TAB: tb.at[3:6, 0, 0:240], SWAP: tb.at[0:3, 0], SWAP2: tb.at[0:2, 0], SWAP3: tb.at[0:3, 0],
            BASE: gb.at[0], OVERZ: mz.at[0:7], COUNT: cg.at[0:15, 0:1], CODE: cr.at[0:15, 0:9], NEWCODE: cr.at[0:15, 0:8],
        }
        for h in range(2):
            sizes |= {CENT + h: r1.at[h], CENT + 2 + h: r2.at[h], CENT + 4 + h: r2.at[h], CENT + 6 + h: r1.at[h]}
        for phase, ref in sizes.items():
            drain(ref, snd.at[phase])


def unload(cent_vm, code_vm, cent_out, code_out, sem):
    a = pltpu.make_async_copy(cent_vm, cent_out, sem.at[0])
    b = pltpu.make_async_copy(code_vm, code_out, sem.at[1])
    a.start()
    b.start()
    a.wait()
    b.wait()


def shards(embeddings, assignment, centroids, codebooks):
    dma = pltpu.SemaphoreType.DMA
    v = pltpu.VMEM
    hbm = pl.BlockSpec(memory_space=pltpu.HBM)
    vm = pl.BlockSpec(memory_space=pltpu.VMEM)
    outs = pl.pallas_call(
        kernel,
        out_shape=(v((KL, D), F32), v((4, 16, 256), F32)),
        in_specs=[hbm] * 4,
        out_specs=(vm, vm),
        scratch_shapes=[
            v((R, D), BF16), pltpu.SMEM((R,), jnp.int32), v((KL, D), BF16), v((4, 16, 256), F32),
            v((KL, R), F32), v((KL, R), BF16),
            v((2, 16, 128), F32), v((2, 16, 128), F32), v((16, 128), F32), v((8, 16, 128), F32), v((2, 16, 128), F32),
            v((2, 16, 128), F32),
            v((3, 16, 128), BF16), v((8, 2, 256, 128), BF16), v((4096, 128), F32), v((R // 2, 128), F32), v((2, R // 2, 128), BF16),
            v((128, R), BF16), v((128, R), BF16), v((4, 256, 128), BF16),
            v((4, 256, 256), F32), v((2, 2, 3, 64, 256), F32), v((4, 64, 256), F32), v((2, 2, 3, 16, 256), F32),
            v((16, 8, 256), F32), v((256, 128), F32), v((4, 256, 256), F32), v((256, 256), F32),
            v((16, 16, 128), F32), v((16, 16, 128), F32),
            v((R, 128), BF16), v((2, 256, RC), F32), v((4, 256, 2 * RC), BF16),
            dma((3 + len(LOADS),)), dma((PHASES,)), dma((PHASES,)),
        ],
        compiler_params=pltpu.CompilerParams(
            collective_id=0, has_side_effects=True, vmem_limit_bytes=60 * 1024 * 1024),
        name="step",
    )(*(pltpu.with_memory_space_constraint(a, pltpu.HBM) for a in (embeddings, assignment, centroids, codebooks)))
    hb = pltpu.HBM
    return pl.pallas_call(
        unload,
        out_shape=(hb((KL, D), F32), hb((4, 16, 256), F32)),
        in_specs=[vm] * 2,
        out_specs=(hbm, hbm),
        scratch_shapes=[dma((2,))],
        name="unload",
    )(*(pltpu.with_memory_space_constraint(a, pltpu.VMEM) for a in outs))


def solution(mesh):
    placed = (P("dp", None), P("dp"), P("sub", None), P("sub", None, None))
    return jax.shard_map(
        shards,
        mesh=mesh,
        in_specs=placed,
        out_specs=(P("sub", None), P("sub", None, None)),
        check_vma=False,
    )
```

```python
import jax
import jax.numpy as jnp
from jax import lax
from jax.experimental import pallas as pl
from jax.experimental.pallas import tpu as pltpu
from jax.sharding import PartitionSpec as P

R, D, KL = 3072, 1024, 256
NC, RC = 6, 512
LOADS = ((0, 512), (512, 1024), (1536, 1024), (2560, 512))
PAIR, ZFAR, ZNEAR, TAB, SWAP, SWAP2, BASE, OVERZ, COUNT, CODE, NEWCODE, CENT = range(12)
SCALE = CENT + 8
PHASES = SCALE + 4
F32, BF16 = jnp.float32, jnp.bfloat16
LOG2E = 1.4426950408889634


def rcopy(src, dst, ssem, rsem, **where):
    return pltpu.make_async_remote_copy(
        src_ref=src, dst_ref=dst, send_sem=ssem, recv_sem=rsem,
        device_id=where, device_id_type=pl.DeviceIdType.MESH,
    )


def drain(ref, sem):
    pltpu.make_async_copy(ref, ref, sem).wait()


def split3(v):
    a = v.astype(BF16).astype(F32)
    r = v - a
    b = r.astype(BF16).astype(F32)
    return a, b, (r - b).astype(BF16).astype(F32)


def kernel(
    emb_hbm, asg_hbm, cent_hbm, cb_hbm, out_ref, cbo_ref,
    emb, asg, cent, cb, eT, wT, ml, st, ra, mz, scl, zbuf, tb, tf, xg, gb, embT, cenT, cbt,
    sums, r1, s1, r2, cg, cc, acc, accT, cs, cr, xgb, lsc, wh, wb, scb,
    lsem, snd, rcv,
):
    dp = lax.axis_index("dp")
    sub = lax.axis_index("sub")
    y, x = dp // 4, dp % 4
    z, c = sub // 2, sub % 2

    def send(phase, src, dst, **where):
        rcopy(src, dst, snd.at[phase], rcv.at[phase], **where).start()

    with jax.named_scope("load"):
        lc = pltpu.make_async_copy(cent_hbm, cent, lsem.at[0])
        lb = pltpu.make_async_copy(cb_hbm, cb, lsem.at[1])
        la = pltpu.make_async_copy(asg_hbm, asg, lsem.at[2])
        lc.start()
        loads = {}
        for k, (r0, n) in enumerate(LOADS):
            cp = pltpu.make_async_copy(emb_hbm.at[r0:r0 + n, :], emb.at[r0:r0 + n, :], lsem.at[3 + k])
            cp.start()
            loads[r0 // RC] = cp
        mz[...] = jnp.zeros(mz.shape, F32)
        bar = pltpu.get_barrier_semaphore()
        for k in range(1, 16):
            pl.semaphore_signal(bar, inc=1, device_id={"sub": (sub + k) % 16}, device_id_type=pl.DeviceIdType.MESH)
            pl.semaphore_signal(bar, inc=1, device_id={"dp": (dp + k) % 16}, device_id_type=pl.DeviceIdType.MESH)
        lb.start()
        la.start()
        st[...] = jnp.zeros(st.shape, F32)
        ml[...] = jnp.zeros(ml.shape, F32)
        rows16 = pl.ds(pl.multiple_of(dp * 16, 16), 16)
        lanes128 = pl.ds(pl.multiple_of(z * 128, 128), 128)

    with jax.named_scope("logits"):
        pad_one = jnp.where(lax.broadcasted_iota(jnp.int32, (2, 16, 128), 1) < 12, 0.0, 1.0)
        lc.wait()
        cf = cent[...].astype(F32)
        hn = 0.5 * jnp.sum(cf * cf, axis=1, keepdims=True)
        for k in range(NC):
            if k in loads:
                loads[k].wait()
            l = lax.dot_general(cent[...], emb[k * RC:(k + 1) * RC, :], (((1,), (1,)), ((), ())),
                                preferred_element_type=F32) - hn
            m = jnp.max(l, axis=0, keepdims=True)
            e = jnp.exp(l - m)
            s = jnp.sum(e, axis=0, keepdims=True)
            eT[:, k * RC:(k + 1) * RC] = e
            for i in range(RC // 128):
                h, r = divmod(k * (RC // 128) + i, 12)
                ml[h, r:r + 1, :] = m[:, i * 128:(i + 1) * 128]
                st[h, r:r + 1, :] = s[:, i * 128:(i + 1) * 128]
        st[...] = ml[...] + jnp.log(st[...] + pad_one)

    with jax.named_scope("barrier"):
        pl.semaphore_wait(bar, 30)
    with jax.named_scope("statsend"):
        other = z * 2 + (1 - c)
        send(PAIR, st.at[1 - c], ra, sub=other)
    with jax.named_scope("zsend"):
        for k in (4, 3, 5, 2, 6):
            zz = (z + k) % 8
            send(ZFAR, cent.at[rows16, pl.ds(pl.multiple_of(zz * 128, 128), 128)], zbuf.at[6 - k], sub=zz * 2 + c)
    with jax.named_scope("cbprep"):
        acc[...] = jnp.zeros(acc.shape, F32)
        tb[0, c] = cent[:, lanes128]
        lb.wait()
        for s in range(4):
            v = cb[s]
            parts = split3(v * LOG2E)
            half = split3(-0.5 * LOG2E * jnp.sum(v * v, axis=0, keepdims=True))
            neg = tuple(-p for p in parts)
            stack = jnp.concatenate(parts + neg + half + (jnp.zeros((29, 256), F32),), axis=0)
            cbt[s] = jnp.transpose(stack).astype(BF16)
        for k in range(NC):
            o = k * RC
            embT[:, pl.ds(o, RC)] = jnp.transpose(emb[pl.ds(o, RC), lanes128].astype(F32)).astype(BF16)

    with jax.named_scope("statwait"):
        drain(ra, rcv.at[PAIR])
    with jax.named_scope("merge"):
        ma, mb = st[c], ra[...]
        big = jnp.maximum(ma, mb)
        mz[c, z] = big + jnp.log(jnp.exp(ma - big) + jnp.exp(mb - big))
        half = mz.at[c, z, 0:12]
        for k in (4, 3, 5, 2, 6, 1, 7):
            for core in range(2):
                send(OVERZ, half, half, sub=((z + k) % 8) * 2 + core)
        send(OVERZ, half, half, sub=other)
        for k in (1, 7):
            zz = (z + k) % 8
            send(ZNEAR, cent.at[:, pl.ds(pl.multiple_of(zz * 128, 128), 128)], tb.at[8 - k, c], sub=zz * 2 + c)
    with jax.named_scope("zwait"):
        drain(zbuf, rcv.at[ZFAR])
    with jax.named_scope("tabsend"):
        tb[2:7, c, rows16] = zbuf[...]
        for j in range(1, 16):
            send(TAB, zbuf, tb.at[2:7, c, rows16], dp=(dp + j) % 16)
    with jax.named_scope("finwait"):
        drain(cr.at[0:15, 0:12], rcv.at[OVERZ])
    with jax.named_scope("merge2"):
        mv = mz[...]
        big = jnp.max(mv, axis=1)
        scl[...] = jnp.exp(ml[...] - (big + jnp.log(jnp.sum(jnp.exp(mv - big[:, None]), axis=1))))
    with jax.named_scope("weights"):
        cp_ = jnp.zeros((KL, 128), F32)
        for k in range(NC):
            scale = []
            for i in range(RC // 128):
                h, r = divmod(k * (RC // 128) + i, 12)
                scale.append(scl[h, r:r + 1, :])
            p = eT[:, k * RC:(k + 1) * RC] * jnp.concatenate(scale, axis=1)
            for i in range(RC // 128):
                cp_ = cp_ + p[:, i * 128:(i + 1) * 128]
            wT[:, k * RC:(k + 1) * RC] = p.astype(BF16)
    def along(i, first, k):
        if (i == 0) == first:
            return y * 4 + (x + k) % 4, (x + k) % 4
        return ((y + k) % 4) * 4 + x, (y + k) % 4

    ax = [(x, y), (y, x)]
    with jax.named_scope("sums"):
        for h in range(2):
            for q in (2 * h, 2 * h + 1):
                sums[q] = jnp.dot(wT[...], emb[:, q * 256:(q + 1) * 256], preferred_element_type=F32)
            for k in (1, 3, 2):
                for i in range(2):
                    dev, pa = along(i, True, k)
                    send(CENT + h, sums.at[2 * h + i, pl.ds(pl.multiple_of(pa * 64, 64), 64), :],
                         r1.at[h, i, k - 1], dp=dev)
            if h == 0:
                drain(tb.at[0:2, 0], rcv.at[ZNEAR])
                send(SWAP, tb.at[0:2, c], tb.at[0:2, c], sub=other)
                send(SWAP, tb.at[7, c], tb.at[7, c], sub=other)
    with jax.named_scope("counts"):
        cg[dp, 0:1, :] = jnp.sum(jnp.transpose(cp_), axis=0, keepdims=True)
        for k in range(1, 16):
            send(COUNT, cg.at[dp, 0:1], cg.at[dp, 0:1], dp=(dp + k) % 16)

    with jax.named_scope("tabwait"):
        drain(tb.at[2:7, 0, 0:240], rcv.at[TAB])
        send(SWAP2, tb.at[2:7, c], tb.at[2:7, c], sub=other)
    with jax.named_scope("swap"):
        drain(tb.at[0:3, 0], rcv.at[SWAP])
        drain(tb.at[0:5, 0], rcv.at[SWAP2])
        la.wait()
    with jax.named_scope("widen"):
        for i in range(8):
            for j in range(2):
                at = pl.multiple_of(((z + i) % 8) * 512 + j * 256, 256)
                tf[pl.ds(at, 256), :] = tb[i, j].astype(F32)
    with jax.named_scope("gather"):
        def fetch(i, _):
            o = pl.multiple_of(i * 128, 128)
            for j in range(128):
                xg[pl.ds(o + j, 1), :] = tf[pl.ds(asg[first + o + j], 1), :]
            return 0
        first = c * (R // 2)
        for k in range(3):
            lax.fori_loop(k * 4, (k + 1) * 4, fetch, 0)
            part = pl.ds(k * RC, RC)
            gb[c, part, :] = xg[part, :].astype(BF16)
            send(BASE, gb.at[c, part], gb.at[c, part], sub=other)

    def block(k):
        return pl.ds(pl.multiple_of(((c + k // 3) % 2 * 3 + k % 3) * RC, RC), RC)

    mine = (lax.broadcasted_iota(jnp.int32, (RC, 128), 1) // 64) == c

    def turn(k):
        g = gb[(c + k // 3) % 2, pl.ds(k % 3 * RC, RC), :].astype(F32)
        cenT[:, block(k)] = jnp.transpose(g).astype(BF16)
        xgb[block(k), :] = jnp.where(mine, g, 1.0).astype(BF16)

    diag = (lax.broadcasted_iota(jnp.int32, (16, 128), 0) == lax.broadcasted_iota(jnp.int32, (16, 128), 1))

    def stage1(h):
        drain(r1.at[h], rcv.at[CENT + h])
        for i in range(2):
            q = 2 * h + i
            s1[q] = (sums[q, pl.ds(pl.multiple_of(ax[i][0] * 64, 64), 64), :]
                     + r1[h, i, 0] + r1[h, i, 1] + r1[h, i, 2])
        for k in (1, 3, 2):
            for i in range(2):
                dev, pb = along(i, False, k)
                send(CENT + 2 + h, s1.at[2 * h + i, pl.ds(pl.multiple_of(pb * 16, 16), 16), :],
                     r2.at[h, i, k - 1], dp=dev)

    def stage2(h):
        drain(r2.at[h], rcv.at[CENT + 2 + h])
        for i in range(2):
            q = 2 * h + i
            a, b = ax[i]
            row = pl.ds(pl.multiple_of(a * 64 + b * 16, 16), 16)
            qs = slice(q * 256, (q + 1) * 256)
            fin = s1[q, pl.ds(pl.multiple_of(b * 16, 16), 16), :] + r2[h, i, 0] + r2[h, i, 1] + r2[h, i, 2]
            den = cc[row, :]
            v = (fin + cent[row, qs].astype(F32)) / jnp.concatenate([den, den], axis=1)
            top = jnp.maximum(jnp.max(jnp.abs(v), axis=1, keepdims=True), 1e-30)
            code_ = jnp.floor(v * (32767.0 / top) + 0.5).astype(jnp.int32)
            wb[h, i, row, :] = (code_[:, 0:128] << 16) | (code_[:, 128:256] & 0xFFFF)
            unit = jnp.broadcast_to(top * (1.0 / 32767.0), (16, 128))
            scb[h, i, a * 4 + b, 0:1, :] = jnp.sum(jnp.where(diag, unit, 0.0), axis=0, keepdims=True)
        for k in (1, 3, 2):
            for i in range(2):
                a, b = ax[i]
                dev = along(i, False, k)[0]
                piece = wb.at[h, i, pl.ds(pl.multiple_of(a * 64 + b * 16, 16), 16)]
                send(CENT + 4 + h, piece, piece, dp=dev)
                piece = scb.at[h, i, a * 4 + b, 0:1]
                send(SCALE + h, piece, piece, dp=dev)

    def stage3(h):
        drain(wb.at[h, 0, 0:96], rcv.at[CENT + 4 + h])
        drain(scb.at[h, 0, 0:6, 0:1], rcv.at[SCALE + h])
        for k in (1, 3, 2):
            for i in range(2):
                dev = along(i, True, k)[0]
                piece = wb.at[h, i, pl.ds(pl.multiple_of(ax[i][0] * 64, 64), 64)]
                send(CENT + 6 + h, piece, piece, dp=dev)
                piece = scb.at[h, i, pl.ds(ax[i][0] * 4, 4), 0:1]
                send(SCALE + 2 + h, piece, piece, dp=dev)

    def stage4(h):
        drain(wb.at[h, :, 0:192], rcv.at[CENT + 6 + h])
        drain(scb.at[h, :, 0:12, 0:1], rcv.at[SCALE + 2 + h])
        for i in range(2):
            q = (2 * h + i) * 256
            for r in range(16):
                rows = slice(r * 16, r * 16 + 16)
                unit = jnp.sum(jnp.where(diag, jnp.broadcast_to(scb[h, i, r, 0:1, :], (16, 128)), 0.0),
                               axis=1, keepdims=True)
                w = wb[h, i, rows, :]
                out_ref[rows, q:q + 128] = (w >> 16).astype(F32) * unit
                out_ref[rows, q + 128:q + 256] = ((w << 16) >> 16).astype(F32) * unit

    one = jnp.ones((16, RC), BF16)

    def code_logits(i):
        k, s = i // 4, i % 4
        cols = block(k)
        f = pl.ds(pl.multiple_of(c * 64 + 16 * s, 16), 16)
        es, cs_ = embT[f, cols], cenT[f, cols]
        xt = jnp.concatenate([es, es, es, cs_, cs_, cs_, one, one], axis=0)
        lsc[i % 2] = jnp.dot(cbt[s], xt, preferred_element_type=F32)

    def code(lo_, hi_):
        for i in range(lo_, hi_):
            k, s = i // 4, i % 4
            if i + 1 < 4 * NC:
                code_logits(i + 1)
            for j in range(RC // 256):
                l = lsc[i % 2, :, j * 256:(j + 1) * 256]
                e = jnp.exp2(l - jnp.max(l, axis=0, keepdims=True))
                w = e * (1.0 / jnp.sum(e, axis=0, keepdims=True))
                hi = w.astype(BF16)
                wh[s, :, j * 256:(j + 1) * 256] = hi
                wh[s, :, RC + j * 256:RC + (j + 1) * 256] = (w - hi.astype(F32)).astype(BF16)
            rows = block(k)
            both = jnp.concatenate([emb[rows, lanes128], xgb[rows, :]], axis=1)
            acc[s] += (jnp.dot(wh[s, :, 0:RC], both, preferred_element_type=F32)
                       + jnp.dot(wh[s, :, RC:2 * RC], both, preferred_element_type=F32))

    def prepare(s):
        accT[s] = jnp.transpose(acc[s])
        f = pl.multiple_of(c * 64 + s * 16, 16)
        tot16 = accT[s, pl.ds(f, 16), :] - accT[s, pl.ds(pl.multiple_of(128 + f, 16), 16), :]
        cnt = accT[s, pl.ds(pl.multiple_of(128 + (1 - c) * 64, 64), 8), :]
        for h in range(2):
            for g in range(2):
                cs[s * 4 + h * 2 + g, 0:8, :] = tot16[8 * g:8 * g + 8, 128 * h:128 * h + 128]
                cs[s * 4 + h * 2 + g, 8:9, :] = cnt[0:1, 128 * h:128 * h + 128]

    with jax.named_scope("code1"):
        for k in range(3):
            turn(k)
        code_logits(0)
        code(0, 4)
    with jax.named_scope("s1A"):
        stage1(0)
    with jax.named_scope("code2"):
        code(4, 11)
    with jax.named_scope("basewait"):
        drain(gb.at[0], rcv.at[BASE])
    with jax.named_scope("code3"):
        for k in range(3, 6):
            turn(k)
        code(11, 13)
    with jax.named_scope("s1B"):
        stage1(1)
    with jax.named_scope("code4"):
        code(13, 17)
    with jax.named_scope("cntwait"):
        drain(cg.at[0:15, 0:1], rcv.at[COUNT])
        ctot = jnp.sum(cg[:, 0:1, :], axis=0)
        cc[...] = jnp.transpose(jnp.broadcast_to(ctot, (128, 256))) + 1.0
    with jax.named_scope("s2A"):
        stage2(0)
    with jax.named_scope("code5"):
        code(17, 21)
        for s in range(3):
            prepare(s)
            code(21 + s, 22 + s)
        prepare(3)
    with jax.named_scope("codeprep"):
        for k in range(1, 16):
            o = (dp + k) % 16
            send(CODE, cs.at[o, 0:9], cr.at[dp, 0:9], dp=o)
        cr[dp, 0:9, :] = cs[dp, 0:9, :]
    with jax.named_scope("s2B"):
        stage2(1)
    with jax.named_scope("s3A"):
        stage3(0)
    with jax.named_scope("s3B"):
        stage3(1)
    with jax.named_scope("codewait"):
        drain(cr.at[0:15, 0:9], rcv.at[CODE])
    with jax.named_scope("codefin"):
        t = jnp.sum(cr[:, 0:8, :], axis=0)
        n = jnp.sum(cr[:, 8:9, :], axis=0)
        so, ho, go = dp // 4, (dp // 2) % 2, dp % 2
        g8 = pl.ds(pl.multiple_of(go * 8, 8), 8)
        h128 = pl.ds(pl.multiple_of(ho * 128, 128), 128)
        cbo_ref[so, g8, h128] = (t + cb[so, g8, h128]) / (n + 1.0)
        for k in range(1, 16):
            piece = cbo_ref.at[so, g8, h128]
            send(NEWCODE, piece, piece, dp=(dp + k) % 16)
    with jax.named_scope("newcent"):
        stage4(0)
        stage4(1)
    with jax.named_scope("newcode"):
        drain(cr.at[0:15, 0:8], rcv.at[NEWCODE])
    with jax.named_scope("sent"):
        sizes = {
            PAIR: ra, ZFAR: zbuf, ZNEAR: tb.at[0:2, 0],
            TAB: tb.at[2:7, 0, 0:240], SWAP: tb.at[0:3, 0], SWAP2: tb.at[0:5, 0],
            BASE: gb.at[0], OVERZ: cr.at[0:15, 0:12], COUNT: cg.at[0:15, 0:1], CODE: cr.at[0:15, 0:9], NEWCODE: cr.at[0:15, 0:8],
        }
        for h in range(2):
            sizes |= {CENT + h: r1.at[h], CENT + 2 + h: r2.at[h], CENT + 4 + h: wb.at[h, 0, 0:96],
                      CENT + 6 + h: wb.at[h, :, 0:192], SCALE + h: scb.at[h, 0, 0:6, 0:1],
                      SCALE + 2 + h: scb.at[h, :, 0:12, 0:1]}
        for phase, ref in sizes.items():
            drain(ref, snd.at[phase])


def unload(cent_vm, code_vm, cent_out, code_out, sem):
    copies = [pltpu.make_async_copy(code_vm, code_out, sem.at[4])]
    for k in range(4):
        rows = pl.ds(k * 64, 64)
        copies.append(pltpu.make_async_copy(cent_vm.at[rows], cent_out.at[rows], sem.at[k]))
    for cp in copies:
        cp.start()
    for cp in copies:
        cp.wait()


def shards(embeddings, assignment, centroids, codebooks):
    dma = pltpu.SemaphoreType.DMA
    v = pltpu.VMEM
    hbm = pl.BlockSpec(memory_space=pltpu.HBM)
    vm = pl.BlockSpec(memory_space=pltpu.VMEM)
    outs = pl.pallas_call(
        kernel,
        out_shape=(v((KL, D), F32), v((4, 16, 256), F32)),
        in_specs=[hbm] * 4,
        out_specs=(vm, vm),
        scratch_shapes=[
            v((R, D), BF16), pltpu.SMEM((R,), jnp.int32), v((KL, D), BF16), v((4, 16, 256), F32),
            v((KL, R), F32), v((KL, R), BF16),
            v((2, 16, 128), F32), v((2, 16, 128), F32), v((16, 128), F32), v((2, 8, 16, 128), F32), v((2, 16, 128), F32),
            v((5, 16, 128), BF16), v((8, 2, 256, 128), BF16), v((4096, 128), F32), v((R // 2, 128), F32), v((2, R // 2, 128), BF16),
            v((128, R), BF16), v((128, R), BF16), v((4, 256, 128), BF16),
            v((4, 256, 256), F32), v((2, 2, 3, 64, 256), F32), v((4, 64, 256), F32), v((2, 2, 3, 16, 256), F32),
            v((16, 8, 256), F32), v((256, 128), F32), v((4, 256, 256), F32), v((4, 256, 256), F32),
            v((16, 16, 128), F32), v((16, 16, 128), F32),
            v((R, 128), BF16), v((2, 256, RC), F32), v((4, 256, 2 * RC), BF16),
            v((2, 2, 256, 128), jnp.int32), v((2, 2, 16, 8, 128), F32),
            dma((3 + len(LOADS),)), dma((PHASES,)), dma((PHASES,)),
        ],
        compiler_params=pltpu.CompilerParams(
            collective_id=0, has_side_effects=True, vmem_limit_bytes=60 * 1024 * 1024),
        name="step",
    )(*(pltpu.with_memory_space_constraint(a, pltpu.HBM) for a in (embeddings, assignment, centroids, codebooks)))
    hb = pltpu.HBM
    return pl.pallas_call(
        unload,
        out_shape=(hb((KL, D), F32), hb((4, 16, 256), F32)),
        in_specs=[vm] * 2,
        out_specs=(hbm, hbm),
        scratch_shapes=[dma((5,))],
        name="unload",
    )(*(pltpu.with_memory_space_constraint(a, pltpu.VMEM) for a in outs))


def solution(mesh):
    placed = (P("dp", None), P("dp"), P("sub", None), P("sub", None, None))
    return jax.shard_map(
        shards,
        mesh=mesh,
        in_specs=placed,
        out_specs=(P("sub", None), P("sub", None, None)),
        check_vma=False,
    )
```

```python
import jax
import jax.numpy as jnp
from jax import lax
from jax.experimental import pallas as pl
from jax.experimental.pallas import tpu as pltpu
from jax.sharding import PartitionSpec as P

R, D, KL = 3072, 1024, 256
NC, RC = 6, 512
LOADS = ((0, 512), (512, 1024), (1536, 1024), (2560, 512))
PAIR, ZFAR, ZNEAR, TAB, SWAP, SWAP2, BASE, OVERZ, COUNT, CODE, NEWCODE, CENT = range(12)
SCALE = CENT + 8
PHASES = SCALE + 4
F32, BF16 = jnp.float32, jnp.bfloat16
LOG2E = 1.4426950408889634


def rcopy(src, dst, ssem, rsem, **where):
    return pltpu.make_async_remote_copy(
        src_ref=src, dst_ref=dst, send_sem=ssem, recv_sem=rsem,
        device_id=where, device_id_type=pl.DeviceIdType.MESH,
    )


def drain(ref, sem):
    pltpu.make_async_copy(ref, ref, sem).wait()


def split3(v):
    a = v.astype(BF16).astype(F32)
    r = v - a
    b = r.astype(BF16).astype(F32)
    return a, b, (r - b).astype(BF16).astype(F32)


def kernel(
    emb_hbm, asg_hbm, cent_hbm, cb_hbm, out_ref, cbo_ref,
    emb, asg, cent, cb, eT, wT, ml, st, ra, mz, scl, zbuf, tb, tf, xg, gb, embT, cenT, cbt,
    sums, r1, s1, r2, cg, cc, acc, accT, cs, cr, xgb, lsc, wh, wb, scb,
    lsem, snd, rcv,
):
    dp = lax.axis_index("dp")
    sub = lax.axis_index("sub")
    y, x = dp // 4, dp % 4
    z, c = sub // 2, sub % 2

    def send(phase, src, dst, **where):
        rcopy(src, dst, snd.at[phase], rcv.at[phase], **where).start()

    with jax.named_scope("load"):
        lc = pltpu.make_async_copy(cent_hbm, cent, lsem.at[0])
        lb = pltpu.make_async_copy(cb_hbm, cb, lsem.at[1])
        la = pltpu.make_async_copy(asg_hbm, asg, lsem.at[2])
        lc.start()
        loads = {}
        for k, (r0, n) in enumerate(LOADS):
            cp = pltpu.make_async_copy(emb_hbm.at[r0:r0 + n, :], emb.at[r0:r0 + n, :], lsem.at[3 + k])
            cp.start()
            loads[r0 // RC] = cp
        mz[...] = jnp.zeros(mz.shape, F32)
        bar = pltpu.get_barrier_semaphore()
        for k in range(1, 16):
            pl.semaphore_signal(bar, inc=1, device_id={"sub": (sub + k) % 16}, device_id_type=pl.DeviceIdType.MESH)
            pl.semaphore_signal(bar, inc=1, device_id={"dp": (dp + k) % 16}, device_id_type=pl.DeviceIdType.MESH)
        lb.start()
        la.start()
        st[...] = jnp.zeros(st.shape, F32)
        ml[...] = jnp.zeros(ml.shape, F32)
        rows16 = pl.ds(pl.multiple_of(dp * 16, 16), 16)
        lanes128 = pl.ds(pl.multiple_of(z * 128, 128), 128)

    with jax.named_scope("logits"):
        pad_one = jnp.where(lax.broadcasted_iota(jnp.int32, (2, 16, 128), 1) < 12, 0.0, 1.0)
        lc.wait()
        cf = cent[...].astype(F32)
        hn = 0.5 * jnp.sum(cf * cf, axis=1, keepdims=True)
        for k in range(NC):
            if k in loads:
                loads[k].wait()
            if k == 3:
                with jax.named_scope("barrier"):
                    pl.semaphore_wait(bar, 30)
                for d in (4, 3, 5, 2, 6):
                    zz = (z + d) % 8
                    send(ZFAR, cent.at[rows16, pl.ds(pl.multiple_of(zz * 128, 128), 128)], zbuf.at[6 - d], sub=zz * 2 + c)
            l = lax.dot_general(cent[...], emb[k * RC:(k + 1) * RC, :], (((1,), (1,)), ((), ())),
                                preferred_element_type=F32) - hn
            m = jnp.max(l, axis=0, keepdims=True)
            e = jnp.exp(l - m)
            s = jnp.sum(e, axis=0, keepdims=True)
            eT[:, k * RC:(k + 1) * RC] = e
            for i in range(RC // 128):
                h, r = divmod(k * (RC // 128) + i, 12)
                ml[h, r:r + 1, :] = m[:, i * 128:(i + 1) * 128]
                st[h, r:r + 1, :] = s[:, i * 128:(i + 1) * 128]
        st[...] = ml[...] + jnp.log(st[...] + pad_one)

    with jax.named_scope("statsend"):
        other = z * 2 + (1 - c)
        send(PAIR, st.at[1 - c], ra, sub=other)
    with jax.named_scope("cbprep"):
        acc[...] = jnp.zeros(acc.shape, F32)
        tb[0, c] = cent[:, lanes128]
        lb.wait()
        for s in range(4):
            v = cb[s]
            parts = split3(v * LOG2E)
            half = split3(-0.5 * LOG2E * jnp.sum(v * v, axis=0, keepdims=True))
            neg = tuple(-p for p in parts)
            stack = jnp.concatenate(parts + neg + half + (jnp.zeros((29, 256), F32),), axis=0)
            cbt[s] = jnp.transpose(stack).astype(BF16)
        for k in range(NC):
            o = k * RC
            embT[:, pl.ds(o, RC)] = jnp.transpose(emb[pl.ds(o, RC), lanes128].astype(F32)).astype(BF16)

    with jax.named_scope("statwait"):
        drain(ra, rcv.at[PAIR])
    with jax.named_scope("merge"):
        ma, mb = st[c], ra[...]
        big = jnp.maximum(ma, mb)
        mz[c, z] = big + jnp.log(jnp.exp(ma - big) + jnp.exp(mb - big))
        half = mz.at[c, z, 0:12]
        for k in (4, 3, 5, 2, 6, 1, 7):
            for core in range(2):
                send(OVERZ, half, half, sub=((z + k) % 8) * 2 + core)
        send(OVERZ, half, half, sub=other)
        for k in (1, 7):
            zz = (z + k) % 8
            send(ZNEAR, cent.at[:, pl.ds(pl.multiple_of(zz * 128, 128), 128)], tb.at[8 - k, c], sub=zz * 2 + c)
    with jax.named_scope("zwait"):
        drain(zbuf, rcv.at[ZFAR])
    with jax.named_scope("tabsend"):
        tb[2:7, c, rows16] = zbuf[...]
        for j in range(1, 16):
            send(TAB, zbuf, tb.at[2:7, c, rows16], dp=(dp + j) % 16)
    with jax.named_scope("finwait"):
        drain(cr.at[0:15, 0:12], rcv.at[OVERZ])
    with jax.named_scope("merge2"):
        mv = mz[...]
        big = jnp.max(mv, axis=1)
        scl[...] = jnp.exp(ml[...] - (big + jnp.log(jnp.sum(jnp.exp(mv - big[:, None]), axis=1))))
    with jax.named_scope("weights"):
        cp_ = jnp.zeros((KL, 128), F32)
        for k in range(NC):
            scale = []
            for i in range(RC // 128):
                h, r = divmod(k * (RC // 128) + i, 12)
                scale.append(scl[h, r:r + 1, :])
            p = eT[:, k * RC:(k + 1) * RC] * jnp.concatenate(scale, axis=1)
            for i in range(RC // 128):
                cp_ = cp_ + p[:, i * 128:(i + 1) * 128]
            wT[:, k * RC:(k + 1) * RC] = p.astype(BF16)
    def along(i, first, k):
        if (i == 0) == first:
            return y * 4 + (x + k) % 4, (x + k) % 4
        return ((y + k) % 4) * 4 + x, (y + k) % 4

    ax = [(x, y), (y, x)]
    with jax.named_scope("sums"):
        for h in range(2):
            for q in (2 * h, 2 * h + 1):
                sums[q] = jnp.dot(wT[...], emb[:, q * 256:(q + 1) * 256], preferred_element_type=F32)
            for k in (1, 3, 2):
                for i in range(2):
                    dev, pa = along(i, True, k)
                    send(CENT + h, sums.at[2 * h + i, pl.ds(pl.multiple_of(pa * 64, 64), 64), :],
                         r1.at[h, i, k - 1], dp=dev)
            if h == 0:
                drain(tb.at[0:2, 0], rcv.at[ZNEAR])
                send(SWAP, tb.at[0:2, c], tb.at[0:2, c], sub=other)
                send(SWAP, tb.at[7, c], tb.at[7, c], sub=other)
    with jax.named_scope("counts"):
        cg[dp, 0:1, :] = jnp.sum(jnp.transpose(cp_), axis=0, keepdims=True)
        for k in range(1, 16):
            send(COUNT, cg.at[dp, 0:1], cg.at[dp, 0:1], dp=(dp + k) % 16)

    with jax.named_scope("tabwait"):
        drain(tb.at[2:7, 0, 0:240], rcv.at[TAB])
        send(SWAP2, tb.at[2:7, c], tb.at[2:7, c], sub=other)
    with jax.named_scope("swap"):
        drain(tb.at[0:3, 0], rcv.at[SWAP])
        drain(tb.at[0:5, 0], rcv.at[SWAP2])
        la.wait()
    with jax.named_scope("widen"):
        for i in range(8):
            for j in range(2):
                at = pl.multiple_of(((z + i) % 8) * 512 + j * 256, 256)
                tf[pl.ds(at, 256), :] = tb[i, j].astype(F32)
    with jax.named_scope("gather"):
        def fetch(i, _):
            o = pl.multiple_of(i * 128, 128)
            for j in range(128):
                xg[pl.ds(o + j, 1), :] = tf[pl.ds(asg[first + o + j], 1), :]
            return 0
        first = c * (R // 2)
        for k in range(3):
            lax.fori_loop(k * 4, (k + 1) * 4, fetch, 0)
            part = pl.ds(k * RC, RC)
            gb[c, part, :] = xg[part, :].astype(BF16)
            send(BASE, gb.at[c, part], gb.at[c, part], sub=other)

    def block(k):
        return pl.ds(pl.multiple_of(((c + k // 3) % 2 * 3 + k % 3) * RC, RC), RC)

    mine = (lax.broadcasted_iota(jnp.int32, (RC, 128), 1) // 64) == c

    def turn(k):
        g = gb[(c + k // 3) % 2, pl.ds(k % 3 * RC, RC), :].astype(F32)
        cenT[:, block(k)] = jnp.transpose(g).astype(BF16)
        xgb[block(k), :] = jnp.where(mine, g, 1.0).astype(BF16)

    diag = (lax.broadcasted_iota(jnp.int32, (16, 128), 0) == lax.broadcasted_iota(jnp.int32, (16, 128), 1))

    def stage1(h):
        drain(r1.at[h], rcv.at[CENT + h])
        for i in range(2):
            q = 2 * h + i
            s1[q] = (sums[q, pl.ds(pl.multiple_of(ax[i][0] * 64, 64), 64), :]
                     + r1[h, i, 0] + r1[h, i, 1] + r1[h, i, 2])
        for k in (1, 3, 2):
            for i in range(2):
                dev, pb = along(i, False, k)
                send(CENT + 2 + h, s1.at[2 * h + i, pl.ds(pl.multiple_of(pb * 16, 16), 16), :],
                     r2.at[h, i, k - 1], dp=dev)

    def stage2(h):
        drain(r2.at[h], rcv.at[CENT + 2 + h])
        for i in range(2):
            q = 2 * h + i
            a, b = ax[i]
            row = pl.ds(pl.multiple_of(a * 64 + b * 16, 16), 16)
            qs = slice(q * 256, (q + 1) * 256)
            fin = s1[q, pl.ds(pl.multiple_of(b * 16, 16), 16), :] + r2[h, i, 0] + r2[h, i, 1] + r2[h, i, 2]
            den = cc[row, :]
            v = (fin + cent[row, qs].astype(F32)) / jnp.concatenate([den, den], axis=1)
            top = jnp.maximum(jnp.max(jnp.abs(v), axis=1, keepdims=True), 1e-30)
            code_ = jnp.floor(v * (32767.0 / top) + 0.5).astype(jnp.int32)
            wb[h, i, row, :] = (code_[:, 0:128] << 16) | (code_[:, 128:256] & 0xFFFF)
            unit = jnp.broadcast_to(top * (1.0 / 32767.0), (16, 128))
            scb[h, i, a * 4 + b, 0:1, :] = jnp.sum(jnp.where(diag, unit, 0.0), axis=0, keepdims=True)
        for k in (1, 3, 2):
            for i in range(2):
                a, b = ax[i]
                dev = along(i, False, k)[0]
                piece = wb.at[h, i, pl.ds(pl.multiple_of(a * 64 + b * 16, 16), 16)]
                send(CENT + 4 + h, piece, piece, dp=dev)
                piece = scb.at[h, i, a * 4 + b, 0:1]
                send(SCALE + h, piece, piece, dp=dev)

    def stage3(h):
        drain(wb.at[h, 0, 0:96], rcv.at[CENT + 4 + h])
        drain(scb.at[h, 0, 0:6, 0:1], rcv.at[SCALE + h])
        for k in (1, 3, 2):
            for i in range(2):
                dev = along(i, True, k)[0]
                piece = wb.at[h, i, pl.ds(pl.multiple_of(ax[i][0] * 64, 64), 64)]
                send(CENT + 6 + h, piece, piece, dp=dev)
                piece = scb.at[h, i, pl.ds(ax[i][0] * 4, 4), 0:1]
                send(SCALE + 2 + h, piece, piece, dp=dev)

    def stage4(h):
        drain(wb.at[h, :, 0:192], rcv.at[CENT + 6 + h])
        drain(scb.at[h, :, 0:12, 0:1], rcv.at[SCALE + 2 + h])
        for i in range(2):
            q = (2 * h + i) * 256
            for r in range(16):
                rows = slice(r * 16, r * 16 + 16)
                unit = jnp.sum(jnp.where(diag, jnp.broadcast_to(scb[h, i, r, 0:1, :], (16, 128)), 0.0),
                               axis=1, keepdims=True)
                w = wb[h, i, rows, :]
                out_ref[rows, q:q + 128] = (w >> 16).astype(F32) * unit
                out_ref[rows, q + 128:q + 256] = ((w << 16) >> 16).astype(F32) * unit

    one = jnp.ones((16, RC), BF16)

    def code_logits(i):
        k, s = i // 4, i % 4
        cols = block(k)
        f = pl.ds(pl.multiple_of(c * 64 + 16 * s, 16), 16)
        es, cs_ = embT[f, cols], cenT[f, cols]
        xt = jnp.concatenate([es, es, es, cs_, cs_, cs_, one, one], axis=0)
        lsc[i % 2] = jnp.dot(cbt[s], xt, preferred_element_type=F32)

    def code(lo_, hi_):
        for i in range(lo_, hi_):
            k, s = i // 4, i % 4
            if i + 1 < 4 * NC:
                code_logits(i + 1)
            for j in range(RC // 256):
                l = lsc[i % 2, :, j * 256:(j + 1) * 256]
                e = jnp.exp2(l - jnp.max(l, axis=0, keepdims=True))
                w = e * (1.0 / jnp.sum(e, axis=0, keepdims=True))
                hi = w.astype(BF16)
                wh[s, :, j * 256:(j + 1) * 256] = hi
                wh[s, :, RC + j * 256:RC + (j + 1) * 256] = (w - hi.astype(F32)).astype(BF16)
            rows = block(k)
            both = jnp.concatenate([emb[rows, lanes128], xgb[rows, :]], axis=1)
            acc[s] += (jnp.dot(wh[s, :, 0:RC], both, preferred_element_type=F32)
                       + jnp.dot(wh[s, :, RC:2 * RC], both, preferred_element_type=F32))

    def prepare(s):
        accT[s] = jnp.transpose(acc[s])
        f = pl.multiple_of(c * 64 + s * 16, 16)
        tot16 = accT[s, pl.ds(f, 16), :] - accT[s, pl.ds(pl.multiple_of(128 + f, 16), 16), :]
        cnt = accT[s, pl.ds(pl.multiple_of(128 + (1 - c) * 64, 64), 8), :]
        for h in range(2):
            for g in range(2):
                cs[s * 4 + h * 2 + g, 0:8, :] = tot16[8 * g:8 * g + 8, 128 * h:128 * h + 128]
                cs[s * 4 + h * 2 + g, 8:9, :] = cnt[0:1, 128 * h:128 * h + 128]

    with jax.named_scope("code1"):
        for k in range(3):
            turn(k)
        code_logits(0)
        code(0, 4)
    with jax.named_scope("s1A"):
        stage1(0)
    with jax.named_scope("code2"):
        code(4, 11)
    with jax.named_scope("basewait"):
        drain(gb.at[0], rcv.at[BASE])
    with jax.named_scope("code3"):
        for k in range(3, 6):
            turn(k)
        code(11, 13)
    with jax.named_scope("s1B"):
        stage1(1)
    with jax.named_scope("code4"):
        code(13, 17)
    with jax.named_scope("cntwait"):
        drain(cg.at[0:15, 0:1], rcv.at[COUNT])
        ctot = jnp.sum(cg[:, 0:1, :], axis=0)
        cc[...] = jnp.transpose(jnp.broadcast_to(ctot, (128, 256))) + 1.0
    with jax.named_scope("s2A"):
        stage2(0)
    with jax.named_scope("code5"):
        code(17, 21)
        for s in range(3):
            prepare(s)
            code(21 + s, 22 + s)
        prepare(3)
    with jax.named_scope("codeprep"):
        for k in range(1, 16):
            o = (dp + k) % 16
            send(CODE, cs.at[o, 0:9], cr.at[dp, 0:9], dp=o)
        cr[dp, 0:9, :] = cs[dp, 0:9, :]
    with jax.named_scope("s2B"):
        stage2(1)
    with jax.named_scope("s3A"):
        stage3(0)
    with jax.named_scope("s3B"):
        stage3(1)
    with jax.named_scope("codewait"):
        drain(cr.at[0:15, 0:9], rcv.at[CODE])
    with jax.named_scope("codefin"):
        t = jnp.sum(cr[:, 0:8, :], axis=0)
        n = jnp.sum(cr[:, 8:9, :], axis=0)
        so, ho, go = dp // 4, (dp // 2) % 2, dp % 2
        g8 = pl.ds(pl.multiple_of(go * 8, 8), 8)
        h128 = pl.ds(pl.multiple_of(ho * 128, 128), 128)
        cbo_ref[so, g8, h128] = (t + cb[so, g8, h128]) / (n + 1.0)
        for k in range(1, 16):
            piece = cbo_ref.at[so, g8, h128]
            send(NEWCODE, piece, piece, dp=(dp + k) % 16)
    with jax.named_scope("newcent"):
        stage4(0)
        stage4(1)
    with jax.named_scope("newcode"):
        drain(cr.at[0:15, 0:8], rcv.at[NEWCODE])
    with jax.named_scope("sent"):
        sizes = {
            PAIR: ra, ZFAR: zbuf, ZNEAR: tb.at[0:2, 0],
            TAB: tb.at[2:7, 0, 0:240], SWAP: tb.at[0:3, 0], SWAP2: tb.at[0:5, 0],
            BASE: gb.at[0], OVERZ: cr.at[0:15, 0:12], COUNT: cg.at[0:15, 0:1], CODE: cr.at[0:15, 0:9], NEWCODE: cr.at[0:15, 0:8],
        }
        for h in range(2):
            sizes |= {CENT + h: r1.at[h], CENT + 2 + h: r2.at[h], CENT + 4 + h: wb.at[h, 0, 0:96],
                      CENT + 6 + h: wb.at[h, :, 0:192], SCALE + h: scb.at[h, 0, 0:6, 0:1],
                      SCALE + 2 + h: scb.at[h, :, 0:12, 0:1]}
        for phase, ref in sizes.items():
            drain(ref, snd.at[phase])


def unload(cent_vm, code_vm, cent_out, code_out, sem):
    copies = [pltpu.make_async_copy(code_vm, code_out, sem.at[4])]
    for k in range(4):
        rows = pl.ds(k * 64, 64)
        copies.append(pltpu.make_async_copy(cent_vm.at[rows], cent_out.at[rows], sem.at[k]))
    for cp in copies:
        cp.start()
    for cp in copies:
        cp.wait()


def shards(embeddings, assignment, centroids, codebooks):
    dma = pltpu.SemaphoreType.DMA
    v = pltpu.VMEM
    hbm = pl.BlockSpec(memory_space=pltpu.HBM)
    vm = pl.BlockSpec(memory_space=pltpu.VMEM)
    outs = pl.pallas_call(
        kernel,
        out_shape=(v((KL, D), F32), v((4, 16, 256), F32)),
        in_specs=[hbm] * 4,
        out_specs=(vm, vm),
        scratch_shapes=[
            v((R, D), BF16), pltpu.SMEM((R,), jnp.int32), v((KL, D), BF16), v((4, 16, 256), F32),
            v((KL, R), F32), v((KL, R), BF16),
            v((2, 16, 128), F32), v((2, 16, 128), F32), v((16, 128), F32), v((2, 8, 16, 128), F32), v((2, 16, 128), F32),
            v((5, 16, 128), BF16), v((8, 2, 256, 128), BF16), v((4096, 128), F32), v((R // 2, 128), F32), v((2, R // 2, 128), BF16),
            v((128, R), BF16), v((128, R), BF16), v((4, 256, 128), BF16),
            v((4, 256, 256), F32), v((2, 2, 3, 64, 256), F32), v((4, 64, 256), F32), v((2, 2, 3, 16, 256), F32),
            v((16, 8, 256), F32), v((256, 128), F32), v((4, 256, 256), F32), v((4, 256, 256), F32),
            v((16, 16, 128), F32), v((16, 16, 128), F32),
            v((R, 128), BF16), v((2, 256, RC), F32), v((4, 256, 2 * RC), BF16),
            v((2, 2, 256, 128), jnp.int32), v((2, 2, 16, 8, 128), F32),
            dma((3 + len(LOADS),)), dma((PHASES,)), dma((PHASES,)),
        ],
        compiler_params=pltpu.CompilerParams(
            collective_id=0, has_side_effects=True, vmem_limit_bytes=60 * 1024 * 1024),
        name="step",
    )(*(pltpu.with_memory_space_constraint(a, pltpu.HBM) for a in (embeddings, assignment, centroids, codebooks)))
    hb = pltpu.HBM
    return pl.pallas_call(
        unload,
        out_shape=(hb((KL, D), F32), hb((4, 16, 256), F32)),
        in_specs=[vm] * 2,
        out_specs=(hbm, hbm),
        scratch_shapes=[dma((5,))],
        name="unload",
    )(*(pltpu.with_memory_space_constraint(a, pltpu.VMEM) for a in outs))


def solution(mesh):
    placed = (P("dp", None), P("dp"), P("sub", None), P("sub", None, None))
    return jax.shard_map(
        shards,
        mesh=mesh,
        in_specs=placed,
        out_specs=(P("sub", None), P("sub", None, None)),
        check_vma=False,
    )
```

```python
import jax
import jax.numpy as jnp
from jax import lax
from jax.experimental import pallas as pl
from jax.experimental.pallas import tpu as pltpu
from jax.sharding import PartitionSpec as P

R, D, KL = 3072, 1024, 256
NC, RC = 6, 512
LOADS = ((0, 512), (512, 1024), (1536, 1024), (2560, 512))
PAIR, ZFAR, ZNEAR, TAB, SWAP, SWAP2, BASE, OVERZ, COUNT, CODE, NEWCODE, CENT = range(12)
SCALE = CENT + 8
PHASES = SCALE + 4
F32, BF16 = jnp.float32, jnp.bfloat16
LOG2E = 1.4426950408889634


def rcopy(src, dst, ssem, rsem, **where):
    return pltpu.make_async_remote_copy(
        src_ref=src, dst_ref=dst, send_sem=ssem, recv_sem=rsem,
        device_id=where, device_id_type=pl.DeviceIdType.MESH,
    )


def drain(ref, sem):
    pltpu.make_async_copy(ref, ref, sem).wait()


def split3(v):
    a = v.astype(BF16).astype(F32)
    r = v - a
    b = r.astype(BF16).astype(F32)
    return a, b, (r - b).astype(BF16).astype(F32)


def kernel(
    emb_hbm, asg_hbm, cent_hbm, cb_hbm, out_ref, cbo_ref,
    emb, asg, cent, cb, eT, wT, ml, st, ra, mz, scl, zbuf, tb, tf, xg, gb, embT, cenT, cbt,
    sums, r1, s1, r2, cg, cc, acc, accT, cs, cr, xgb, lsc, wh, wb, scb,
    lsem, snd, rcv,
):
    dp = lax.axis_index("dp")
    sub = lax.axis_index("sub")
    y, x = dp // 4, dp % 4
    z, c = sub // 2, sub % 2

    def send(phase, src, dst, **where):
        rcopy(src, dst, snd.at[phase], rcv.at[phase], **where).start()

    with jax.named_scope("load"):
        lc = pltpu.make_async_copy(cent_hbm, cent, lsem.at[0])
        lb = pltpu.make_async_copy(cb_hbm, cb, lsem.at[1])
        la = pltpu.make_async_copy(asg_hbm, asg, lsem.at[2])
        lc.start()
        loads = {}
        for k, (r0, n) in enumerate(LOADS):
            cp = pltpu.make_async_copy(emb_hbm.at[r0:r0 + n, :], emb.at[r0:r0 + n, :], lsem.at[3 + k])
            cp.start()
            loads[r0 // RC] = cp
        mz[...] = jnp.zeros(mz.shape, F32)
        bar = pltpu.get_barrier_semaphore()
        for k in range(1, 16):
            pl.semaphore_signal(bar, inc=1, device_id={"sub": (sub + k) % 16}, device_id_type=pl.DeviceIdType.MESH)
            pl.semaphore_signal(bar, inc=1, device_id={"dp": (dp + k) % 16}, device_id_type=pl.DeviceIdType.MESH)
        lb.start()
        la.start()
        st[...] = jnp.zeros(st.shape, F32)
        ml[...] = jnp.zeros(ml.shape, F32)
        rows16 = pl.ds(pl.multiple_of(dp * 16, 16), 16)
        lanes128 = pl.ds(pl.multiple_of(z * 128, 128), 128)

    with jax.named_scope("logits"):
        pad_one = jnp.where(lax.broadcasted_iota(jnp.int32, (2, 16, 128), 1) < 12, 0.0, 1.0)
        lc.wait()
        cf = cent[...].astype(F32)
        hn = 0.5 * jnp.sum(cf * cf, axis=1, keepdims=True)
        for k in range(NC):
            if k in loads:
                loads[k].wait()
            if k == 3:
                with jax.named_scope("barrier"):
                    pl.semaphore_wait(bar, 30)
                for d in (4, 3, 5, 2, 6):
                    zz = (z + d) % 8
                    send(ZFAR, cent.at[rows16, pl.ds(pl.multiple_of(zz * 128, 128), 128)], zbuf.at[6 - d], sub=zz * 2 + c)
                for d in (1, 7):
                    zz = (z + d) % 8
                    send(ZNEAR, cent.at[:, pl.ds(pl.multiple_of(zz * 128, 128), 128)], tb.at[8 - d, c], sub=zz * 2 + c)
            l = lax.dot_general(cent[...], emb[k * RC:(k + 1) * RC, :], (((1,), (1,)), ((), ())),
                                preferred_element_type=F32) - hn
            m = jnp.max(l, axis=0, keepdims=True)
            e = jnp.exp(l - m)
            s = jnp.sum(e, axis=0, keepdims=True)
            eT[:, k * RC:(k + 1) * RC] = e
            for i in range(RC // 128):
                h, r = divmod(k * (RC // 128) + i, 12)
                ml[h, r:r + 1, :] = m[:, i * 128:(i + 1) * 128]
                st[h, r:r + 1, :] = s[:, i * 128:(i + 1) * 128]
        st[...] = ml[...] + jnp.log(st[...] + pad_one)

    with jax.named_scope("statsend"):
        other = z * 2 + (1 - c)
        send(PAIR, st.at[1 - c], ra, sub=other)
    with jax.named_scope("cbprep"):
        acc[...] = jnp.zeros(acc.shape, F32)
        tb[0, c] = cent[:, lanes128]
        lb.wait()
        for s in range(4):
            v = cb[s]
            parts = split3(v * LOG2E)
            half = split3(-0.5 * LOG2E * jnp.sum(v * v, axis=0, keepdims=True))
            neg = tuple(-p for p in parts)
            stack = jnp.concatenate(parts + neg + half + (jnp.zeros((29, 256), F32),), axis=0)
            cbt[s] = jnp.transpose(stack).astype(BF16)
        for k in range(NC):
            o = k * RC
            embT[:, pl.ds(o, RC)] = jnp.transpose(emb[pl.ds(o, RC), lanes128].astype(F32)).astype(BF16)

    with jax.named_scope("statwait"):
        drain(ra, rcv.at[PAIR])
    with jax.named_scope("merge"):
        ma, mb = st[c], ra[...]
        big = jnp.maximum(ma, mb)
        mz[c, z] = big + jnp.log(jnp.exp(ma - big) + jnp.exp(mb - big))
        half = mz.at[c, z, 0:12]
        for k in (4, 3, 5, 2, 6, 1, 7):
            for core in range(2):
                send(OVERZ, half, half, sub=((z + k) % 8) * 2 + core)
        send(OVERZ, half, half, sub=other)
    with jax.named_scope("zwait"):
        drain(zbuf, rcv.at[ZFAR])
    with jax.named_scope("tabsend"):
        tb[2:7, c, rows16] = zbuf[...]
        for j in range(1, 16):
            send(TAB, zbuf, tb.at[2:7, c, rows16], dp=(dp + j) % 16)
    with jax.named_scope("finwait"):
        drain(cr.at[0:15, 0:12], rcv.at[OVERZ])
    with jax.named_scope("merge2"):
        mv = mz[...]
        big = jnp.max(mv, axis=1)
        scl[...] = jnp.exp(ml[...] - (big + jnp.log(jnp.sum(jnp.exp(mv - big[:, None]), axis=1))))
    with jax.named_scope("weights"):
        cp_ = jnp.zeros((KL, 128), F32)
        for k in range(NC):
            scale = []
            for i in range(RC // 128):
                h, r = divmod(k * (RC // 128) + i, 12)
                scale.append(scl[h, r:r + 1, :])
            p = eT[:, k * RC:(k + 1) * RC] * jnp.concatenate(scale, axis=1)
            for i in range(RC // 128):
                cp_ = cp_ + p[:, i * 128:(i + 1) * 128]
            wT[:, k * RC:(k + 1) * RC] = p.astype(BF16)
    def along(i, first, k):
        if (i == 0) == first:
            return y * 4 + (x + k) % 4, (x + k) % 4
        return ((y + k) % 4) * 4 + x, (y + k) % 4

    ax = [(x, y), (y, x)]
    with jax.named_scope("sums"):
        for h in range(2):
            for q in (2 * h, 2 * h + 1):
                sums[q] = jnp.dot(wT[...], emb[:, q * 256:(q + 1) * 256], preferred_element_type=F32)
            for k in (1, 3, 2):
                for i in range(2):
                    dev, pa = along(i, True, k)
                    send(CENT + h, sums.at[2 * h + i, pl.ds(pl.multiple_of(pa * 64, 64), 64), :],
                         r1.at[h, i, k - 1], dp=dev)
            if h == 0:
                drain(tb.at[0:2, 0], rcv.at[ZNEAR])
                send(SWAP, tb.at[0:2, c], tb.at[0:2, c], sub=other)
                send(SWAP, tb.at[7, c], tb.at[7, c], sub=other)
    with jax.named_scope("counts"):
        cg[dp, 0:1, :] = jnp.sum(jnp.transpose(cp_), axis=0, keepdims=True)
        for k in range(1, 16):
            send(COUNT, cg.at[dp, 0:1], cg.at[dp, 0:1], dp=(dp + k) % 16)

    with jax.named_scope("tabwait"):
        drain(tb.at[2:7, 0, 0:240], rcv.at[TAB])
        send(SWAP2, tb.at[2:7, c], tb.at[2:7, c], sub=other)
    with jax.named_scope("swap"):
        drain(tb.at[0:3, 0], rcv.at[SWAP])
        drain(tb.at[0:5, 0], rcv.at[SWAP2])
        la.wait()
    with jax.named_scope("widen"):
        for i in range(8):
            for j in range(2):
                at = pl.multiple_of(((z + i) % 8) * 512 + j * 256, 256)
                tf[pl.ds(at, 256), :] = tb[i, j].astype(F32)
    with jax.named_scope("gather"):
        def fetch(i, _):
            o = pl.multiple_of(i * 128, 128)
            for j in range(128):
                xg[pl.ds(o + j, 1), :] = tf[pl.ds(asg[first + o + j], 1), :]
            return 0
        first = c * (R // 2)
        for k in range(3):
            lax.fori_loop(k * 4, (k + 1) * 4, fetch, 0)
            part = pl.ds(k * RC, RC)
            gb[c, part, :] = xg[part, :].astype(BF16)
            send(BASE, gb.at[c, part], gb.at[c, part], sub=other)

    def block(k):
        return pl.ds(pl.multiple_of(((c + k // 3) % 2 * 3 + k % 3) * RC, RC), RC)

    mine = (lax.broadcasted_iota(jnp.int32, (RC, 128), 1) // 64) == c

    def turn(k):
        g = gb[(c + k // 3) % 2, pl.ds(k % 3 * RC, RC), :].astype(F32)
        cenT[:, block(k)] = jnp.transpose(g).astype(BF16)
        xgb[block(k), :] = jnp.where(mine, g, 1.0).astype(BF16)

    diag = (lax.broadcasted_iota(jnp.int32, (16, 128), 0) == lax.broadcasted_iota(jnp.int32, (16, 128), 1))

    def stage1(h):
        drain(r1.at[h], rcv.at[CENT + h])
        for i in range(2):
            q = 2 * h + i
            s1[q] = (sums[q, pl.ds(pl.multiple_of(ax[i][0] * 64, 64), 64), :]
                     + r1[h, i, 0] + r1[h, i, 1] + r1[h, i, 2])
        for k in (1, 3, 2):
            for i in range(2):
                dev, pb = along(i, False, k)
                send(CENT + 2 + h, s1.at[2 * h + i, pl.ds(pl.multiple_of(pb * 16, 16), 16), :],
                     r2.at[h, i, k - 1], dp=dev)

    def stage2(h):
        drain(r2.at[h], rcv.at[CENT + 2 + h])
        for i in range(2):
            q = 2 * h + i
            a, b = ax[i]
            row = pl.ds(pl.multiple_of(a * 64 + b * 16, 16), 16)
            qs = slice(q * 256, (q + 1) * 256)
            fin = s1[q, pl.ds(pl.multiple_of(b * 16, 16), 16), :] + r2[h, i, 0] + r2[h, i, 1] + r2[h, i, 2]
            den = cc[row, :]
            v = (fin + cent[row, qs].astype(F32)) / jnp.concatenate([den, den], axis=1)
            top = jnp.maximum(jnp.max(jnp.abs(v), axis=1, keepdims=True), 1e-30)
            code_ = jnp.floor(v * (32767.0 / top) + 0.5).astype(jnp.int32)
            wb[h, i, row, :] = (code_[:, 0:128] << 16) | (code_[:, 128:256] & 0xFFFF)
            unit = jnp.broadcast_to(top * (1.0 / 32767.0), (16, 128))
            scb[h, i, a * 4 + b, 0:1, :] = jnp.sum(jnp.where(diag, unit, 0.0), axis=0, keepdims=True)
        for k in (1, 3, 2):
            for i in range(2):
                a, b = ax[i]
                dev = along(i, False, k)[0]
                piece = wb.at[h, i, pl.ds(pl.multiple_of(a * 64 + b * 16, 16), 16)]
                send(CENT + 4 + h, piece, piece, dp=dev)
                piece = scb.at[h, i, a * 4 + b, 0:1]
                send(SCALE + h, piece, piece, dp=dev)

    def stage3(h):
        drain(wb.at[h, 0, 0:96], rcv.at[CENT + 4 + h])
        drain(scb.at[h, 0, 0:6, 0:1], rcv.at[SCALE + h])
        for k in (1, 3, 2):
            for i in range(2):
                dev = along(i, True, k)[0]
                piece = wb.at[h, i, pl.ds(pl.multiple_of(ax[i][0] * 64, 64), 64)]
                send(CENT + 6 + h, piece, piece, dp=dev)
                piece = scb.at[h, i, pl.ds(ax[i][0] * 4, 4), 0:1]
                send(SCALE + 2 + h, piece, piece, dp=dev)

    def stage4(h):
        drain(wb.at[h, :, 0:192], rcv.at[CENT + 6 + h])
        drain(scb.at[h, :, 0:12, 0:1], rcv.at[SCALE + 2 + h])
        for i in range(2):
            q = (2 * h + i) * 256
            for r in range(16):
                rows = slice(r * 16, r * 16 + 16)
                unit = jnp.sum(jnp.where(diag, jnp.broadcast_to(scb[h, i, r, 0:1, :], (16, 128)), 0.0),
                               axis=1, keepdims=True)
                w = wb[h, i, rows, :]
                out_ref[rows, q:q + 128] = (w >> 16).astype(F32) * unit
                out_ref[rows, q + 128:q + 256] = ((w << 16) >> 16).astype(F32) * unit

    one = jnp.ones((16, RC), BF16)

    def code_logits(i):
        k, s = i // 4, i % 4
        cols = block(k)
        f = pl.ds(pl.multiple_of(c * 64 + 16 * s, 16), 16)
        es, cs_ = embT[f, cols], cenT[f, cols]
        xt = jnp.concatenate([es, es, es, cs_, cs_, cs_, one, one], axis=0)
        lsc[i % 2] = jnp.dot(cbt[s], xt, preferred_element_type=F32)

    def code(lo_, hi_):
        for i in range(lo_, hi_):
            k, s = i // 4, i % 4
            if i + 1 < 4 * NC:
                code_logits(i + 1)
            for j in range(RC // 256):
                l = lsc[i % 2, :, j * 256:(j + 1) * 256]
                e = jnp.exp2(l - jnp.max(l, axis=0, keepdims=True))
                w = e * (1.0 / jnp.sum(e, axis=0, keepdims=True))
                hi = w.astype(BF16)
                wh[s, :, j * 256:(j + 1) * 256] = hi
                wh[s, :, RC + j * 256:RC + (j + 1) * 256] = (w - hi.astype(F32)).astype(BF16)
            rows = block(k)
            both = jnp.concatenate([emb[rows, lanes128], xgb[rows, :]], axis=1)
            acc[s] += (jnp.dot(wh[s, :, 0:RC], both, preferred_element_type=F32)
                       + jnp.dot(wh[s, :, RC:2 * RC], both, preferred_element_type=F32))

    def prepare(s):
        accT[s] = jnp.transpose(acc[s])
        f = pl.multiple_of(c * 64 + s * 16, 16)
        tot16 = accT[s, pl.ds(f, 16), :] - accT[s, pl.ds(pl.multiple_of(128 + f, 16), 16), :]
        cnt = accT[s, pl.ds(pl.multiple_of(128 + (1 - c) * 64, 64), 8), :]
        for h in range(2):
            for g in range(2):
                cs[s * 4 + h * 2 + g, 0:8, :] = tot16[8 * g:8 * g + 8, 128 * h:128 * h + 128]
                cs[s * 4 + h * 2 + g, 8:9, :] = cnt[0:1, 128 * h:128 * h + 128]

    with jax.named_scope("code1"):
        for k in range(3):
            turn(k)
        code_logits(0)
        code(0, 4)
    with jax.named_scope("s1A"):
        stage1(0)
    with jax.named_scope("code2"):
        code(4, 11)
    with jax.named_scope("basewait"):
        drain(gb.at[0], rcv.at[BASE])
    with jax.named_scope("code3"):
        for k in range(3, 6):
            turn(k)
        code(11, 13)
    with jax.named_scope("s1B"):
        stage1(1)
    with jax.named_scope("code4"):
        code(13, 17)
    with jax.named_scope("cntwait"):
        drain(cg.at[0:15, 0:1], rcv.at[COUNT])
        ctot = jnp.sum(cg[:, 0:1, :], axis=0)
        cc[...] = jnp.transpose(jnp.broadcast_to(ctot, (128, 256))) + 1.0
    with jax.named_scope("s2A"):
        stage2(0)
    with jax.named_scope("code5"):
        code(17, 21)
        for s in range(3):
            prepare(s)
            code(21 + s, 22 + s)
        prepare(3)
    with jax.named_scope("codeprep"):
        for k in range(1, 16):
            o = (dp + k) % 16
            send(CODE, cs.at[o, 0:9], cr.at[dp, 0:9], dp=o)
        cr[dp, 0:9, :] = cs[dp, 0:9, :]
    with jax.named_scope("s2B"):
        stage2(1)
    with jax.named_scope("s3A"):
        stage3(0)
    with jax.named_scope("s3B"):
        stage3(1)
    with jax.named_scope("codewait"):
        drain(cr.at[0:15, 0:9], rcv.at[CODE])
    with jax.named_scope("codefin"):
        t = jnp.sum(cr[:, 0:8, :], axis=0)
        n = jnp.sum(cr[:, 8:9, :], axis=0)
        so, ho, go = dp // 4, (dp // 2) % 2, dp % 2
        g8 = pl.ds(pl.multiple_of(go * 8, 8), 8)
        h128 = pl.ds(pl.multiple_of(ho * 128, 128), 128)
        cbo_ref[so, g8, h128] = (t + cb[so, g8, h128]) / (n + 1.0)
        for k in range(1, 16):
            piece = cbo_ref.at[so, g8, h128]
            send(NEWCODE, piece, piece, dp=(dp + k) % 16)
    with jax.named_scope("newcent"):
        stage4(0)
        stage4(1)
    with jax.named_scope("newcode"):
        drain(cr.at[0:15, 0:8], rcv.at[NEWCODE])
    with jax.named_scope("sent"):
        sizes = {
            PAIR: ra, ZFAR: zbuf, ZNEAR: tb.at[0:2, 0],
            TAB: tb.at[2:7, 0, 0:240], SWAP: tb.at[0:3, 0], SWAP2: tb.at[0:5, 0],
            BASE: gb.at[0], OVERZ: cr.at[0:15, 0:12], COUNT: cg.at[0:15, 0:1], CODE: cr.at[0:15, 0:9], NEWCODE: cr.at[0:15, 0:8],
        }
        for h in range(2):
            sizes |= {CENT + h: r1.at[h], CENT + 2 + h: r2.at[h], CENT + 4 + h: wb.at[h, 0, 0:96],
                      CENT + 6 + h: wb.at[h, :, 0:192], SCALE + h: scb.at[h, 0, 0:6, 0:1],
                      SCALE + 2 + h: scb.at[h, :, 0:12, 0:1]}
        for phase, ref in sizes.items():
            drain(ref, snd.at[phase])


def unload(cent_vm, code_vm, cent_out, code_out, sem):
    copies = [pltpu.make_async_copy(code_vm, code_out, sem.at[4])]
    for k in range(4):
        rows = pl.ds(k * 64, 64)
        copies.append(pltpu.make_async_copy(cent_vm.at[rows], cent_out.at[rows], sem.at[k]))
    for cp in copies:
        cp.start()
    for cp in copies:
        cp.wait()


def shards(embeddings, assignment, centroids, codebooks):
    dma = pltpu.SemaphoreType.DMA
    v = pltpu.VMEM
    hbm = pl.BlockSpec(memory_space=pltpu.HBM)
    vm = pl.BlockSpec(memory_space=pltpu.VMEM)
    outs = pl.pallas_call(
        kernel,
        out_shape=(v((KL, D), F32), v((4, 16, 256), F32)),
        in_specs=[hbm] * 4,
        out_specs=(vm, vm),
        scratch_shapes=[
            v((R, D), BF16), pltpu.SMEM((R,), jnp.int32), v((KL, D), BF16), v((4, 16, 256), F32),
            v((KL, R), F32), v((KL, R), BF16),
            v((2, 16, 128), F32), v((2, 16, 128), F32), v((16, 128), F32), v((2, 8, 16, 128), F32), v((2, 16, 128), F32),
            v((5, 16, 128), BF16), v((8, 2, 256, 128), BF16), v((4096, 128), F32), v((R // 2, 128), F32), v((2, R // 2, 128), BF16),
            v((128, R), BF16), v((128, R), BF16), v((4, 256, 128), BF16),
            v((4, 256, 256), F32), v((2, 2, 3, 64, 256), F32), v((4, 64, 256), F32), v((2, 2, 3, 16, 256), F32),
            v((16, 8, 256), F32), v((256, 128), F32), v((4, 256, 256), F32), v((4, 256, 256), F32),
            v((16, 16, 128), F32), v((16, 16, 128), F32),
            v((R, 128), BF16), v((2, 256, RC), F32), v((4, 256, 2 * RC), BF16),
            v((2, 2, 256, 128), jnp.int32), v((2, 2, 16, 8, 128), F32),
            dma((3 + len(LOADS),)), dma((PHASES,)), dma((PHASES,)),
        ],
        compiler_params=pltpu.CompilerParams(
            collective_id=0, has_side_effects=True, vmem_limit_bytes=60 * 1024 * 1024),
        name="step",
    )(*(pltpu.with_memory_space_constraint(a, pltpu.HBM) for a in (embeddings, assignment, centroids, codebooks)))
    hb = pltpu.HBM
    return pl.pallas_call(
        unload,
        out_shape=(hb((KL, D), F32), hb((4, 16, 256), F32)),
        in_specs=[vm] * 2,
        out_specs=(hbm, hbm),
        scratch_shapes=[dma((5,))],
        name="unload",
    )(*(pltpu.with_memory_space_constraint(a, pltpu.VMEM) for a in outs))


def solution(mesh):
    placed = (P("dp", None), P("dp"), P("sub", None), P("sub", None, None))
    return jax.shard_map(
        shards,
        mesh=mesh,
        in_specs=placed,
        out_specs=(P("sub", None), P("sub", None, None)),
        check_vma=False,
    )
```

```python
import jax
import jax.numpy as jnp
from jax import lax
from jax.experimental import pallas as pl
from jax.experimental.pallas import tpu as pltpu
from jax.sharding import PartitionSpec as P

R, D, KL = 3072, 1024, 256
NC, RC = 6, 512
LOADS = ((0, 512), (512, 1024), (1536, 1024), (2560, 512))
PAIR, ZFAR, ZNEAR, TAB, SWAP, SWAP2, BASE, OVERZ, COUNT, CODE, NEWCODE, CENT = range(12)
SCALE = CENT + 8
PHASES = SCALE + 4
F32, BF16 = jnp.float32, jnp.bfloat16
FAR_FIRST = sorted(
    ((i % 4, i // 4) for i in range(1, 16)), key=lambda v: -sum(min(k, 4 - k) for k in v))
LOG2E = 1.4426950408889634


def rcopy(src, dst, ssem, rsem, **where):
    return pltpu.make_async_remote_copy(
        src_ref=src, dst_ref=dst, send_sem=ssem, recv_sem=rsem,
        device_id=where, device_id_type=pl.DeviceIdType.MESH,
    )


def drain(ref, sem):
    pltpu.make_async_copy(ref, ref, sem).wait()


def split3(v):
    a = v.astype(BF16).astype(F32)
    r = v - a
    b = r.astype(BF16).astype(F32)
    return a, b, (r - b).astype(BF16).astype(F32)


def kernel(
    emb_hbm, asg_hbm, cent_hbm, cb_hbm, out_ref, cbo_ref,
    emb, asg, cent, cb, eT, wT, ml, st, ra, mz, scl, zbuf, tb, tf, xg, gb, embT, cenT, cbt,
    sums, r1, s1, r2, cg, cc, acc, accT, cs, cr, xgb, lsc, wh, wb, scb,
    lsem, snd, rcv,
):
    dp = lax.axis_index("dp")
    sub = lax.axis_index("sub")
    y, x = dp // 4, dp % 4
    z, c = sub // 2, sub % 2

    others = [((y + ky) % 4) * 4 + (x + kx) % 4 for kx, ky in FAR_FIRST]

    def send(phase, src, dst, **where):
        rcopy(src, dst, snd.at[phase], rcv.at[phase], **where).start()

    with jax.named_scope("load"):
        lc = pltpu.make_async_copy(cent_hbm, cent, lsem.at[0])
        lb = pltpu.make_async_copy(cb_hbm, cb, lsem.at[1])
        la = pltpu.make_async_copy(asg_hbm, asg, lsem.at[2])
        lc.start()
        loads = {}
        for k, (r0, n) in enumerate(LOADS):
            cp = pltpu.make_async_copy(emb_hbm.at[r0:r0 + n, :], emb.at[r0:r0 + n, :], lsem.at[3 + k])
            cp.start()
            loads[r0 // RC] = cp
        mz[...] = jnp.zeros(mz.shape, F32)
        bar = pltpu.get_barrier_semaphore()
        for k in range(1, 16):
            pl.semaphore_signal(bar, inc=1, device_id={"sub": (sub + k) % 16}, device_id_type=pl.DeviceIdType.MESH)
            pl.semaphore_signal(bar, inc=1, device_id={"dp": (dp + k) % 16}, device_id_type=pl.DeviceIdType.MESH)
        lb.start()
        la.start()
        st[...] = jnp.zeros(st.shape, F32)
        ml[...] = jnp.zeros(ml.shape, F32)
        rows16 = pl.ds(pl.multiple_of(dp * 16, 16), 16)
        lanes128 = pl.ds(pl.multiple_of(z * 128, 128), 128)

    with jax.named_scope("logits"):
        pad_one = jnp.where(lax.broadcasted_iota(jnp.int32, (2, 16, 128), 1) < 12, 0.0, 1.0)
        lc.wait()
        cf = cent[...].astype(F32)
        hn = 0.5 * jnp.sum(cf * cf, axis=1, keepdims=True)
        for k in range(NC):
            if k in loads:
                loads[k].wait()
            if k == 3:
                with jax.named_scope("barrier"):
                    pl.semaphore_wait(bar, 30)
                for d in (4, 3, 5, 2, 6):
                    zz = (z + d) % 8
                    send(ZFAR, cent.at[rows16, pl.ds(pl.multiple_of(zz * 128, 128), 128)], zbuf.at[6 - d], sub=zz * 2 + c)
            l = lax.dot_general(cent[...], emb[k * RC:(k + 1) * RC, :], (((1,), (1,)), ((), ())),
                                preferred_element_type=F32) - hn
            m = jnp.max(l, axis=0, keepdims=True)
            e = jnp.exp(l - m)
            s = jnp.sum(e, axis=0, keepdims=True)
            eT[:, k * RC:(k + 1) * RC] = e
            for i in range(RC // 128):
                h, r = divmod(k * (RC // 128) + i, 12)
                ml[h, r:r + 1, :] = m[:, i * 128:(i + 1) * 128]
                st[h, r:r + 1, :] = s[:, i * 128:(i + 1) * 128]
        st[...] = ml[...] + jnp.log(st[...] + pad_one)

    with jax.named_scope("statsend"):
        other = z * 2 + (1 - c)
        send(PAIR, st.at[1 - c], ra, sub=other)
    with jax.named_scope("cbprep"):
        acc[...] = jnp.zeros(acc.shape, F32)
        tb[0, c] = cent[:, lanes128]
        lb.wait()
        for s in range(4):
            v = cb[s]
            parts = split3(v * LOG2E)
            half = split3(-0.5 * LOG2E * jnp.sum(v * v, axis=0, keepdims=True))
            neg = tuple(-p for p in parts)
            stack = jnp.concatenate(parts + neg + half + (jnp.zeros((29, 256), F32),), axis=0)
            cbt[s] = jnp.transpose(stack).astype(BF16)
        for k in range(NC):
            o = k * RC
            embT[:, pl.ds(o, RC)] = jnp.transpose(emb[pl.ds(o, RC), lanes128].astype(F32)).astype(BF16)

    with jax.named_scope("statwait"):
        drain(ra, rcv.at[PAIR])
    with jax.named_scope("merge"):
        ma, mb = st[c], ra[...]
        big = jnp.maximum(ma, mb)
        mz[c, z] = big + jnp.log(jnp.exp(ma - big) + jnp.exp(mb - big))
        half = mz.at[c, z, 0:12]
        for k in (4, 3, 5, 2, 6, 1, 7):
            for core in range(2):
                send(OVERZ, half, half, sub=((z + k) % 8) * 2 + core)
        send(OVERZ, half, half, sub=other)
        for k in (1, 7):
            zz = (z + k) % 8
            send(ZNEAR, cent.at[:, pl.ds(pl.multiple_of(zz * 128, 128), 128)], tb.at[8 - k, c], sub=zz * 2 + c)
    with jax.named_scope("zwait"):
        drain(zbuf, rcv.at[ZFAR])
    with jax.named_scope("tabsend"):
        tb[2:7, c, rows16] = zbuf[...]
        for o in others:
            send(TAB, zbuf, tb.at[2:7, c, rows16], dp=o)
    with jax.named_scope("finwait"):
        drain(cr.at[0:15, 0:12], rcv.at[OVERZ])
    with jax.named_scope("merge2"):
        mv = mz[...]
        big = jnp.max(mv, axis=1)
        scl[...] = jnp.exp(ml[...] - (big + jnp.log(jnp.sum(jnp.exp(mv - big[:, None]), axis=1))))
    with jax.named_scope("weights"):
        cp_ = jnp.zeros((KL, 128), F32)
        for k in range(NC):
            scale = []
            for i in range(RC // 128):
                h, r = divmod(k * (RC // 128) + i, 12)
                scale.append(scl[h, r:r + 1, :])
            p = eT[:, k * RC:(k + 1) * RC] * jnp.concatenate(scale, axis=1)
            for i in range(RC // 128):
                cp_ = cp_ + p[:, i * 128:(i + 1) * 128]
            wT[:, k * RC:(k + 1) * RC] = p.astype(BF16)
    def along(i, first, k):
        if (i == 0) == first:
            return y * 4 + (x + k) % 4, (x + k) % 4
        return ((y + k) % 4) * 4 + x, (y + k) % 4

    ax = [(x, y), (y, x)]
    with jax.named_scope("sums"):
        for h in range(2):
            for q in (2 * h, 2 * h + 1):
                sums[q] = jnp.dot(wT[...], emb[:, q * 256:(q + 1) * 256], preferred_element_type=F32)
            for k in (1, 3, 2):
                for i in range(2):
                    dev, pa = along(i, True, k)
                    send(CENT + h, sums.at[2 * h + i, pl.ds(pl.multiple_of(pa * 64, 64), 64), :],
                         r1.at[h, i, k - 1], dp=dev)
            if h == 0:
                drain(tb.at[0:2, 0], rcv.at[ZNEAR])
                send(SWAP, tb.at[0:2, c], tb.at[0:2, c], sub=other)
                send(SWAP, tb.at[7, c], tb.at[7, c], sub=other)
    with jax.named_scope("counts"):
        cg[dp, 0:1, :] = jnp.sum(jnp.transpose(cp_), axis=0, keepdims=True)
        for o in others:
            send(COUNT, cg.at[dp, 0:1], cg.at[dp, 0:1], dp=o)

    with jax.named_scope("tabwait"):
        drain(tb.at[2:7, 0, 0:240], rcv.at[TAB])
        send(SWAP2, tb.at[2:7, c], tb.at[2:7, c], sub=other)
    with jax.named_scope("swap"):
        drain(tb.at[0:3, 0], rcv.at[SWAP])
        drain(tb.at[0:5, 0], rcv.at[SWAP2])
        la.wait()
    with jax.named_scope("widen"):
        for i in range(8):
            for j in range(2):
                at = pl.multiple_of(((z + i) % 8) * 512 + j * 256, 256)
                tf[pl.ds(at, 256), :] = tb[i, j].astype(F32)
    with jax.named_scope("gather"):
        def fetch(i, _):
            o = pl.multiple_of(i * 128, 128)
            for j in range(128):
                xg[pl.ds(o + j, 1), :] = tf[pl.ds(asg[first + o + j], 1), :]
            return 0
        first = c * (R // 2)
        for k in range(3):
            lax.fori_loop(k * 4, (k + 1) * 4, fetch, 0)
            part = pl.ds(k * RC, RC)
            gb[c, part, :] = xg[part, :].astype(BF16)
            send(BASE, gb.at[c, part], gb.at[c, part], sub=other)

    def block(k):
        return pl.ds(pl.multiple_of(((c + k // 3) % 2 * 3 + k % 3) * RC, RC), RC)

    mine = (lax.broadcasted_iota(jnp.int32, (RC, 128), 1) // 64) == c

    def turn(k):
        g = gb[(c + k // 3) % 2, pl.ds(k % 3 * RC, RC), :].astype(F32)
        cenT[:, block(k)] = jnp.transpose(g).astype(BF16)
        xgb[block(k), :] = jnp.where(mine, g, 1.0).astype(BF16)

    diag = (lax.broadcasted_iota(jnp.int32, (16, 128), 0) == lax.broadcasted_iota(jnp.int32, (16, 128), 1))

    def stage1(h):
        drain(r1.at[h], rcv.at[CENT + h])
        for i in range(2):
            q = 2 * h + i
            s1[q] = (sums[q, pl.ds(pl.multiple_of(ax[i][0] * 64, 64), 64), :]
                     + r1[h, i, 0] + r1[h, i, 1] + r1[h, i, 2])
        for k in (1, 3, 2):
            for i in range(2):
                dev, pb = along(i, False, k)
                send(CENT + 2 + h, s1.at[2 * h + i, pl.ds(pl.multiple_of(pb * 16, 16), 16), :],
                     r2.at[h, i, k - 1], dp=dev)

    def stage2(h):
        drain(r2.at[h], rcv.at[CENT + 2 + h])
        for i in range(2):
            q = 2 * h + i
            a, b = ax[i]
            row = pl.ds(pl.multiple_of(a * 64 + b * 16, 16), 16)
            qs = slice(q * 256, (q + 1) * 256)
            fin = s1[q, pl.ds(pl.multiple_of(b * 16, 16), 16), :] + r2[h, i, 0] + r2[h, i, 1] + r2[h, i, 2]
            den = cc[row, :]
            v = (fin + cent[row, qs].astype(F32)) / jnp.concatenate([den, den], axis=1)
            top = jnp.maximum(jnp.max(jnp.abs(v), axis=1, keepdims=True), 1e-30)
            code_ = jnp.floor(v * (32767.0 / top) + 0.5).astype(jnp.int32)
            wb[h, i, row, :] = (code_[:, 0:128] << 16) | (code_[:, 128:256] & 0xFFFF)
            unit = jnp.broadcast_to(top * (1.0 / 32767.0), (16, 128))
            scb[h, i, a * 4 + b, 0:1, :] = jnp.sum(jnp.where(diag, unit, 0.0), axis=0, keepdims=True)
        for k in (1, 3, 2):
            for i in range(2):
                a, b = ax[i]
                dev = along(i, False, k)[0]
                piece = wb.at[h, i, pl.ds(pl.multiple_of(a * 64 + b * 16, 16), 16)]
                send(CENT + 4 + h, piece, piece, dp=dev)
                piece = scb.at[h, i, a * 4 + b, 0:1]
                send(SCALE + h, piece, piece, dp=dev)

    def stage3(h):
        drain(wb.at[h, 0, 0:96], rcv.at[CENT + 4 + h])
        drain(scb.at[h, 0, 0:6, 0:1], rcv.at[SCALE + h])
        for k in (1, 3, 2):
            for i in range(2):
                dev = along(i, True, k)[0]
                piece = wb.at[h, i, pl.ds(pl.multiple_of(ax[i][0] * 64, 64), 64)]
                send(CENT + 6 + h, piece, piece, dp=dev)
                piece = scb.at[h, i, pl.ds(ax[i][0] * 4, 4), 0:1]
                send(SCALE + 2 + h, piece, piece, dp=dev)

    def stage4(h):
        drain(wb.at[h, :, 0:192], rcv.at[CENT + 6 + h])
        drain(scb.at[h, :, 0:12, 0:1], rcv.at[SCALE + 2 + h])
        for i in range(2):
            q = (2 * h + i) * 256
            for r in range(16):
                rows = slice(r * 16, r * 16 + 16)
                unit = jnp.sum(jnp.where(diag, jnp.broadcast_to(scb[h, i, r, 0:1, :], (16, 128)), 0.0),
                               axis=1, keepdims=True)
                w = wb[h, i, rows, :]
                out_ref[rows, q:q + 128] = (w >> 16).astype(F32) * unit
                out_ref[rows, q + 128:q + 256] = ((w << 16) >> 16).astype(F32) * unit

    one = jnp.ones((16, RC), BF16)

    def code_logits(i):
        k, s = i // 4, i % 4
        cols = block(k)
        f = pl.ds(pl.multiple_of(c * 64 + 16 * s, 16), 16)
        es, cs_ = embT[f, cols], cenT[f, cols]
        xt = jnp.concatenate([es, es, es, cs_, cs_, cs_, one, one], axis=0)
        lsc[i % 2] = jnp.dot(cbt[s], xt, preferred_element_type=F32)

    def code(lo_, hi_):
        for i in range(lo_, hi_):
            k, s = i // 4, i % 4
            if i + 1 < 4 * NC:
                code_logits(i + 1)
            for j in range(RC // 256):
                l = lsc[i % 2, :, j * 256:(j + 1) * 256]
                e = jnp.exp2(l - jnp.max(l, axis=0, keepdims=True))
                w = e * (1.0 / jnp.sum(e, axis=0, keepdims=True))
                hi = w.astype(BF16)
                wh[s, :, j * 256:(j + 1) * 256] = hi
                wh[s, :, RC + j * 256:RC + (j + 1) * 256] = (w - hi.astype(F32)).astype(BF16)
            rows = block(k)
            both = jnp.concatenate([emb[rows, lanes128], xgb[rows, :]], axis=1)
            acc[s] += (jnp.dot(wh[s, :, 0:RC], both, preferred_element_type=F32)
                       + jnp.dot(wh[s, :, RC:2 * RC], both, preferred_element_type=F32))

    def prepare(s):
        accT[s] = jnp.transpose(acc[s])
        f = pl.multiple_of(c * 64 + s * 16, 16)
        tot16 = accT[s, pl.ds(f, 16), :] - accT[s, pl.ds(pl.multiple_of(128 + f, 16), 16), :]
        cnt = accT[s, pl.ds(pl.multiple_of(128 + (1 - c) * 64, 64), 8), :]
        for h in range(2):
            for g in range(2):
                cs[s * 4 + h * 2 + g, 0:8, :] = tot16[8 * g:8 * g + 8, 128 * h:128 * h + 128]
                cs[s * 4 + h * 2 + g, 8:9, :] = cnt[0:1, 128 * h:128 * h + 128]

    with jax.named_scope("code1"):
        for k in range(3):
            turn(k)
        code_logits(0)
        code(0, 4)
    with jax.named_scope("s1A"):
        stage1(0)
    with jax.named_scope("code2"):
        code(4, 11)
    with jax.named_scope("basewait"):
        drain(gb.at[0], rcv.at[BASE])
    with jax.named_scope("code3"):
        for k in range(3, 6):
            turn(k)
        code(11, 13)
    with jax.named_scope("s1B"):
        stage1(1)
    with jax.named_scope("code4"):
        code(13, 17)
    with jax.named_scope("cntwait"):
        drain(cg.at[0:15, 0:1], rcv.at[COUNT])
        ctot = jnp.sum(cg[:, 0:1, :], axis=0)
        cc[...] = jnp.transpose(jnp.broadcast_to(ctot, (128, 256))) + 1.0
    with jax.named_scope("s2A"):
        stage2(0)
    with jax.named_scope("code5"):
        code(17, 21)
        for s in range(3):
            prepare(s)
            code(21 + s, 22 + s)
        prepare(3)
    with jax.named_scope("codeprep"):
        for o in others:
            send(CODE, cs.at[o, 0:9], cr.at[dp, 0:9], dp=o)
        cr[dp, 0:9, :] = cs[dp, 0:9, :]
    with jax.named_scope("s2B"):
        stage2(1)
    with jax.named_scope("s3A"):
        stage3(0)
    with jax.named_scope("s3B"):
        stage3(1)
    with jax.named_scope("codewait"):
        drain(cr.at[0:15, 0:9], rcv.at[CODE])
    with jax.named_scope("codefin"):
        t = jnp.sum(cr[:, 0:8, :], axis=0)
        n = jnp.sum(cr[:, 8:9, :], axis=0)
        so, ho, go = dp // 4, (dp // 2) % 2, dp % 2
        g8 = pl.ds(pl.multiple_of(go * 8, 8), 8)
        h128 = pl.ds(pl.multiple_of(ho * 128, 128), 128)
        cbo_ref[so, g8, h128] = (t + cb[so, g8, h128]) / (n + 1.0)
        for o in others:
            piece = cbo_ref.at[so, g8, h128]
            send(NEWCODE, piece, piece, dp=o)
    with jax.named_scope("newcent"):
        stage4(0)
        stage4(1)
    with jax.named_scope("newcode"):
        drain(cr.at[0:15, 0:8], rcv.at[NEWCODE])
    with jax.named_scope("sent"):
        sizes = {
            PAIR: ra, ZFAR: zbuf, ZNEAR: tb.at[0:2, 0],
            TAB: tb.at[2:7, 0, 0:240], SWAP: tb.at[0:3, 0], SWAP2: tb.at[0:5, 0],
            BASE: gb.at[0], OVERZ: cr.at[0:15, 0:12], COUNT: cg.at[0:15, 0:1], CODE: cr.at[0:15, 0:9], NEWCODE: cr.at[0:15, 0:8],
        }
        for h in range(2):
            sizes |= {CENT + h: r1.at[h], CENT + 2 + h: r2.at[h], CENT + 4 + h: wb.at[h, 0, 0:96],
                      CENT + 6 + h: wb.at[h, :, 0:192], SCALE + h: scb.at[h, 0, 0:6, 0:1],
                      SCALE + 2 + h: scb.at[h, :, 0:12, 0:1]}
        for phase, ref in sizes.items():
            drain(ref, snd.at[phase])


def unload(cent_vm, code_vm, cent_out, code_out, sem):
    copies = [pltpu.make_async_copy(code_vm, code_out, sem.at[4])]
    for k in range(4):
        rows = pl.ds(k * 64, 64)
        copies.append(pltpu.make_async_copy(cent_vm.at[rows], cent_out.at[rows], sem.at[k]))
    for cp in copies:
        cp.start()
    for cp in copies:
        cp.wait()


def shards(embeddings, assignment, centroids, codebooks):
    dma = pltpu.SemaphoreType.DMA
    v = pltpu.VMEM
    hbm = pl.BlockSpec(memory_space=pltpu.HBM)
    vm = pl.BlockSpec(memory_space=pltpu.VMEM)
    outs = pl.pallas_call(
        kernel,
        out_shape=(v((KL, D), F32), v((4, 16, 256), F32)),
        in_specs=[hbm] * 4,
        out_specs=(vm, vm),
        scratch_shapes=[
            v((R, D), BF16), pltpu.SMEM((R,), jnp.int32), v((KL, D), BF16), v((4, 16, 256), F32),
            v((KL, R), F32), v((KL, R), BF16),
            v((2, 16, 128), F32), v((2, 16, 128), F32), v((16, 128), F32), v((2, 8, 16, 128), F32), v((2, 16, 128), F32),
            v((5, 16, 128), BF16), v((8, 2, 256, 128), BF16), v((4096, 128), F32), v((R // 2, 128), F32), v((2, R // 2, 128), BF16),
            v((128, R), BF16), v((128, R), BF16), v((4, 256, 128), BF16),
            v((4, 256, 256), F32), v((2, 2, 3, 64, 256), F32), v((4, 64, 256), F32), v((2, 2, 3, 16, 256), F32),
            v((16, 8, 256), F32), v((256, 128), F32), v((4, 256, 256), F32), v((4, 256, 256), F32),
            v((16, 16, 128), F32), v((16, 16, 128), F32),
            v((R, 128), BF16), v((2, 256, RC), F32), v((4, 256, 2 * RC), BF16),
            v((2, 2, 256, 128), jnp.int32), v((2, 2, 16, 8, 128), F32),
            dma((3 + len(LOADS),)), dma((PHASES,)), dma((PHASES,)),
        ],
        compiler_params=pltpu.CompilerParams(
            collective_id=0, has_side_effects=True, vmem_limit_bytes=60 * 1024 * 1024),
        name="step",
    )(*(pltpu.with_memory_space_constraint(a, pltpu.HBM) for a in (embeddings, assignment, centroids, codebooks)))
    hb = pltpu.HBM
    return pl.pallas_call(
        unload,
        out_shape=(hb((KL, D), F32), hb((4, 16, 256), F32)),
        in_specs=[vm] * 2,
        out_specs=(hbm, hbm),
        scratch_shapes=[dma((5,))],
        name="unload",
    )(*(pltpu.with_memory_space_constraint(a, pltpu.VMEM) for a in outs))


def solution(mesh):
    placed = (P("dp", None), P("dp"), P("sub", None), P("sub", None, None))
    return jax.shard_map(
        shards,
        mesh=mesh,
        in_specs=placed,
        out_specs=(P("sub", None), P("sub", None, None)),
        check_vma=False,
    )
```
